256 devices in a mesh: pool: 16 (over z, core), tensor: 16 (over y, x).
Axes of the slice: x: 4, y: 4, z: 8, core: 2. Of those that a mesh axis runs over, the one named last changes fastest.
Arguments:
- hidden: bfloat16 [8192, 14336], P('pool', 'tensor'), may hold values from -6 to 6
- down_weight: bfloat16 [14336, 8192], P('tensor', 'pool'), may hold values from -0.046875 to 0.046875
- adapter_shrink: bfloat16 [32, 14336, 64], P('pool', 'tensor'), may hold values from -0.046875 to 0.046875
- adapter_expand: bfloat16 [32, 8192, 64], P('pool', 'tensor'), may hold values from -0.75 to 0.75
- block_adapter: int32 [64], P('pool'), may hold values from 0 to 31, as said below
- block_rows: int32 [64], P('pool'), may hold values from 1 to 128, 6144 in all
Outputs:
- projected: bfloat16 [8192, 8192], P(('pool', 'tensor'))
The draws below stay inside these ranges and needn't reach their ends.
Inputs may be any that keep to these rules, and one draw needn't show every extreme that they name: `block_adapter`: within each aligned run of 4 blocks (the rows of one pool index) no two blocks name adapters with the same a // 2. `block_rows`: some block is full.
All inputs are finite; a program needn't handle non-finite values.
Results may differ from the reference program's by a relative error of at most 0.02.
Values may be sent and summed in bfloat16 or wider, within the bound.
A program may use at most 128 MiB of HBM per device.

```python
import math
import jax
import jax.numpy as jnp
import numpy as np
from jax import lax

D = 8192
FF = 14336
RANK = 64
ADP_DEV = 2
BLOCK = 128
ROWS = 512
ADAPTERS = 32
TOKENS = 8192
BLOCKS = 64
N_TENSOR = 16


def draw_block_adapter(key, part):
    groups = TOKENS // ROWS
    per_group = ROWS // BLOCK
    holders = ADAPTERS // ADP_DEV
    key_heat, key_noise, key_local = jax.random.split(jax.random.fold_in(key, 7), 3)
    heat = jax.random.randint(key_heat, (holders,), 0, 4)
    noise = jax.random.randint(key_noise, (groups, holders), 0, 1024)
    scores = (noise + heat[None, :] * 512) * holders + jnp.arange(holders, dtype=jnp.int32)[None, :]
    picked = lax.top_k(scores, per_group)[1].astype(jnp.int32)
    local = jax.random.randint(key_local, (groups, per_group), 0, ADP_DEV)
    return (picked * ADP_DEV + local).reshape(-1).astype(jnp.int32)


def block_scale(key, shape, shards, least, largest):
    def one(dim, shards_of):
        steps = jax.random.uniform(jax.random.fold_in(jax.random.fold_in(key, 6), dim), (shards_of,), jnp.float32, least / len(shards), largest / len(shards))
        return jnp.repeat(jnp.exp(steps), shape[dim] // shards_of).reshape((-1,) + (1,) * (len(shape) - dim - 1))

    gain = one(*shards[0])
    for cut in shards[1:]:
        gain = gain * one(*cut)
    return gain


def split_up(number_of, total, most, lean):
    portions = [(1 << 20) // math.isqrt(standing ** lean) + 1 for standing in range(2, number_of + 1)]
    surplus, holding = total - most - (number_of - 1), [1] * (number_of - 1)
    while surplus > 0:
        candidates = [i for i in range(number_of - 1) if holding[i] < most]
        pool, remaining = sum([portions[i] for i in candidates]), surplus
        for i in candidates:
            extra = min(most - holding[i], max(1, remaining * portions[i] // pool), surplus)
            holding[i] = holding[i] + extra
            surplus = surplus - extra
    return np.array([most] + holding)


def ragged_sizes(rng, count, total, bound, lean):
    if count == 2:
        one = jax.random.randint(rng, (), max(1, total - bound), min(bound, total - 1) + 1)
        return jnp.stack([one, total - one])
    tallies = jnp.asarray(split_up(count, total, bound, lean), jnp.int32)
    couples = (count - 1) // 2
    giver, sink = tallies[1:1 + 2 * couples:2], tallies[2:2 + 2 * couples:2]
    room = jnp.minimum(giver - 1, bound - sink)
    moved = jax.random.randint(jax.random.fold_in(rng, 1), (couples,), 0, 1 << 20) % (room + 1)
    tallies = tallies.at[1:1 + 2 * couples:2].set(giver - moved).at[2:2 + 2 * couples:2].set(sink + moved)
    return tallies[jax.random.permutation(jax.random.fold_in(rng, 2), count)]


def scatter_about(own_key, extent, scale, most, cuts=(), kind=jnp.bfloat16):
    drawn = scale * jax.random.normal(own_key, extent, jnp.float32)
    if cuts:
        drawn = drawn * block_scale(own_key, extent, cuts, -0.22, 0.18)
    return jnp.clip(drawn, -most, most).astype(kind)


def setup_inputs(seed: int = 0) -> dict:
    splits = jax.random.split(jax.random.key(seed), 7)
    return {
        "hidden": scatter_about(splits[0], (TOKENS, FF), 1.0, 6.0, ((0, 16), (1, 16))),
        "down_weight": scatter_about(splits[1], (FF, D), FF ** -0.5, 0.046875, ((0, 16), (1, 16))),
        "adapter_shrink": scatter_about(splits[2], (ADAPTERS, FF, RANK), FF ** -0.5, 0.046875, ((0, 16), (1, 16))),
        "adapter_expand": scatter_about(splits[3], (ADAPTERS, D, RANK), RANK ** -0.5, 0.75, ((0, 16), (1, 16))),
        "block_adapter": draw_block_adapter(jax.random.fold_in(splits[6], 71), 0),
        "block_rows": ragged_sizes(splits[5], BLOCKS, BLOCKS * BLOCK * 3 // 4, BLOCK, 1).astype(jnp.int32),
    }


adapter_scale_factor = 0.5


def reference(hidden, down_weight, adapter_shrink, adapter_expand, block_adapter, block_rows):
    def one_block(item):
        block_vals, ident = item
        ident = ident.astype(jnp.int32)
        shrink_w = lax.dynamic_index_in_dim(adapter_shrink, ident, 0, keepdims=False)
        expand_w = lax.dynamic_index_in_dim(adapter_expand, ident, 0, keepdims=False)
        shrink = jnp.dot(block_vals, shrink_w, preferred_element_type=jnp.float32).astype(jnp.bfloat16)
        enlarged_rows = jnp.dot(shrink, expand_w.T, preferred_element_type=jnp.float32)
        return (adapter_scale_factor * enlarged_rows).astype(jnp.bfloat16)

    delta = lax.map(one_block, (hidden.reshape(BLOCKS, BLOCK, FF), block_adapter)).reshape(TOKENS, D)
    width = FF // N_TENSOR

    def add_term(step, total):
        start = (step * width).astype(jnp.int32)
        columns = lax.dynamic_slice_in_dim(hidden, start, width, 1)
        weight_rows = lax.dynamic_slice_in_dim(down_weight, start, width, 0)
        term = jnp.dot(columns, weight_rows, preferred_element_type=jnp.float32)
        rounded_length = lax.optimization_barrier(term.astype(jnp.bfloat16))
        return total + rounded_length.astype(jnp.float32)

    total = lax.fori_loop(0, N_TENSOR, add_term, jnp.zeros((TOKENS, D), jnp.float32))
    total = total + delta.astype(jnp.float32)
    valid = (jnp.arange(TOKENS, dtype=jnp.int32) % BLOCK) < jnp.repeat(block_rows, BLOCK)
    return (total * valid[:, None].astype(jnp.float32)).astype(jnp.bfloat16)
```

```python
import jax
import jax.numpy as jnp
from jax import lax
from jax.sharding import PartitionSpec as P

BLOCK = 128


adapter_scale_factor = 0.5


def tensor_allsum(x, count):
    step = 1
    while step < count:
        perm = [(i, i ^ step) for i in range(count)]
        x = x + lax.ppermute(x, "tensor", perm)
        step *= 2
    return x


def shards(hidden, down_weight, adapter_shrink, adapter_expand, block_adapter, block_rows):
    input_rows, feat = hidden.shape
    block_count = block_adapter.shape[0]
    pool_count = lax.axis_size("pool")
    tensor_pos = lax.axis_index("tensor")
    tensor_count = lax.axis_size("tensor")
    own_rows = input_rows // tensor_count
    held, _, rank = adapter_shrink.shape
    column_span = adapter_expand.shape[1]
    width = down_weight.shape[1]

    shrink_rows = held * feat * rank // width
    expand_rows = held * column_span * rank // width
    pack = jnp.concatenate(
        [
            down_weight,
            adapter_shrink.reshape(shrink_rows, width),
            adapter_expand.reshape(expand_rows, width),
        ],
        axis=0,
    )
    gathered = lax.all_gather(pack, "pool", axis=0, tiled=False)
    w_all = gathered[:, :feat, :]
    shrink_all = gathered[:, feat:feat + shrink_rows, :].reshape(pool_count * held, feat, rank)
    expand_all = gathered[:, feat + shrink_rows:, :].reshape(pool_count * held, column_span, rank)

    first = jnp.take(shrink_all, block_adapter, axis=0)
    second = jnp.take(expand_all, block_adapter, axis=0)
    blocks = hidden.reshape(block_count, BLOCK, feat)
    shrink = jnp.einsum("bnf,bfr->bnr", blocks, first, preferred_element_type=jnp.float32)
    summed_shrink = tensor_allsum(shrink, tensor_count).astype(jnp.bfloat16)
    enlarged_rows = jnp.einsum(
        "bnr,bcr->bnc", summed_shrink, second, preferred_element_type=jnp.float32
    )
    delta = (adapter_scale_factor * enlarged_rows).astype(jnp.bfloat16).reshape(input_rows, column_span)

    partial_value = jnp.einsum("if,pfj->ipj", hidden, w_all, preferred_element_type=jnp.float32)
    chunk_ids = jnp.arange(pool_count, dtype=jnp.int32)[None, :, None]
    partial_value = partial_value + jnp.where(
        chunk_ids == tensor_pos, delta.astype(jnp.float32)[:, None, :], 0.0
    )
    partial_value = partial_value.astype(jnp.bfloat16).reshape(input_rows, pool_count * width)
    total = lax.psum_scatter(partial_value, "tensor", scatter_dimension=0, tiled=True)

    row_ids = tensor_pos * own_rows + jnp.arange(own_rows, dtype=jnp.int32)
    owning = (row_ids // BLOCK)[:, None] == jnp.arange(block_count, dtype=jnp.int32)[None, :]
    lengths = jnp.sum(jnp.where(owning, block_rows[None, :], 0), axis=1)
    valid = row_ids % BLOCK < lengths
    return jnp.where(valid[:, None], total, jnp.zeros_like(total))


def solution(mesh):
    in_specs = (
        P("pool", "tensor"),
        P("tensor", "pool"),
        P("pool", "tensor", None),
        P("pool", "tensor", None),
        P("pool"),
        P("pool"),
    )
    out_specs = P(("pool", "tensor"), None)
    return jax.shard_map(shards, mesh=mesh, in_specs=in_specs, out_specs=out_specs, check_vma=False)
```

```python
import functools

import jax
import jax.numpy as jnp
from jax import lax
from jax.experimental import pallas as pl
from jax.experimental.pallas import tpu as pltpu
from jax.sharding import PartitionSpec as P

BLOCK = 128


adapter_scale_factor = 0.5


def tensor_allsum(x, count):
    step = 1
    while step < count:
        perm = [(i, i ^ step) for i in range(count)]
        x = x + lax.ppermute(x, "tensor", perm)
        step *= 2
    return x


def scatter_kernel(count, rows, part_ref, recv_ref, send_sems, recv_sems):
    me = lax.axis_index("tensor")
    pool_me = lax.axis_index("pool")
    barrier = pltpu.get_barrier_semaphore()
    for d in range(1, count):
        other = lax.rem(me + d, count)
        pl.semaphore_signal(
            barrier, 1, device_id=(pool_me, other), device_id_type=pl.DeviceIdType.MESH
        )
    pl.semaphore_wait(barrier, count - 1)
    copies = []
    for d in range(1, count):
        target = lax.rem(me + d, count)
        start = pl.multiple_of(target * rows, rows)
        copy = pltpu.make_async_remote_copy(
            src_ref=part_ref.at[:, pl.ds(start, rows), :],
            dst_ref=recv_ref.at[d - 1],
            send_sem=send_sems.at[d - 1],
            recv_sem=recv_sems.at[d - 1],
            device_id=(pool_me, target),
            device_id_type=pl.DeviceIdType.MESH,
        )
        copy.start()
        copies.append(copy)
    for copy in copies:
        copy.wait()


def scatter_rows(partial_value, count, rows):
    chunks, _, width = partial_value.shape
    return pl.pallas_call(
        functools.partial(scatter_kernel, count, rows),
        out_shape=jax.ShapeDtypeStruct((count - 1, chunks, rows, width), partial_value.dtype),
        in_specs=[pl.BlockSpec(memory_space=pl.ANY)],
        out_specs=pl.BlockSpec(memory_space=pl.ANY),
        scratch_shapes=[
            pltpu.SemaphoreType.DMA((count - 1,)),
            pltpu.SemaphoreType.DMA((count - 1,)),
        ],
        compiler_params=pltpu.CompilerParams(collective_id=0, has_side_effects=True),
    )(partial_value)


def shards(hidden, down_weight, adapter_shrink, adapter_expand, block_adapter, block_rows):
    input_rows, feat = hidden.shape
    block_count = block_adapter.shape[0]
    pool_count = lax.axis_size("pool")
    tensor_pos = lax.axis_index("tensor")
    tensor_count = lax.axis_size("tensor")
    own_rows = input_rows // tensor_count
    held, _, rank = adapter_shrink.shape
    column_span = adapter_expand.shape[1]
    width = down_weight.shape[1]

    shrink_rows = held * feat * rank // width
    expand_rows = held * column_span * rank // width
    pack = jnp.concatenate(
        [
            down_weight,
            adapter_shrink.reshape(shrink_rows, width),
            adapter_expand.reshape(expand_rows, width),
        ],
        axis=0,
    )
    gathered = lax.all_gather(pack, "pool", axis=0, tiled=False)
    w_all = gathered[:, :feat, :]
    shrink_all = gathered[:, feat:feat + shrink_rows, :].reshape(
        pool_count * held, shrink_rows // held, width
    )
    expand_all = gathered[:, feat + shrink_rows:, :].reshape(
        pool_count * held, expand_rows // held, width
    )

    first = jnp.take(shrink_all, block_adapter, axis=0).reshape(block_count, feat, rank)
    second = jnp.take(expand_all, block_adapter, axis=0).reshape(block_count, column_span, rank)
    blocks = hidden.reshape(block_count, BLOCK, feat)
    shrink = jnp.einsum("bnf,bfr->bnr", blocks, first, preferred_element_type=jnp.float32)
    summed_shrink = tensor_allsum(shrink, tensor_count).astype(jnp.bfloat16)
    enlarged_rows = jnp.einsum(
        "bnr,bcr->bnc", summed_shrink, second, preferred_element_type=jnp.float32
    )
    delta = (adapter_scale_factor * enlarged_rows).astype(jnp.bfloat16).reshape(input_rows, column_span)

    partial_value = jnp.einsum("if,pfj->pij", hidden, w_all, preferred_element_type=jnp.float32)
    chunk_ids = jnp.arange(pool_count, dtype=jnp.int32)[:, None, None]
    partial_value = partial_value + jnp.where(
        chunk_ids == tensor_pos, delta.astype(jnp.float32)[None, :, :], 0.0
    )
    partial_value = partial_value.astype(jnp.bfloat16)
    received = scatter_rows(partial_value, tensor_count, own_rows)
    own = lax.dynamic_slice_in_dim(partial_value, tensor_pos * own_rows, own_rows, axis=1)
    total = own.astype(jnp.float32) + jnp.sum(received.astype(jnp.float32), axis=0)
    total = jnp.transpose(total, (1, 0, 2)).reshape(own_rows, pool_count * width)

    row_ids = tensor_pos * own_rows + jnp.arange(own_rows, dtype=jnp.int32)
    owning = (row_ids // BLOCK)[:, None] == jnp.arange(block_count, dtype=jnp.int32)[None, :]
    lengths = jnp.sum(jnp.where(owning, block_rows[None, :], 0), axis=1)
    valid = row_ids % BLOCK < lengths
    return jnp.where(valid[:, None], total, 0.0).astype(jnp.bfloat16)


def solution(mesh):
    in_specs = (
        P("pool", "tensor"),
        P("tensor", "pool"),
        P("pool", "tensor", None),
        P("pool", "tensor", None),
        P("pool"),
        P("pool"),
    )
    out_specs = P(("pool", "tensor"), None)
    return jax.shard_map(shards, mesh=mesh, in_specs=in_specs, out_specs=out_specs, check_vma=False)
```

```python
import functools

import jax
import jax.numpy as jnp
from jax import lax
from jax.experimental import pallas as pl
from jax.experimental.pallas import tpu as pltpu
from jax.sharding import PartitionSpec as P

BLOCK = 128


adapter_scale_factor = 0.5


def tensor_allsum(x, count):
    step = 1
    while step < count:
        perm = [(i, i ^ step) for i in range(count)]
        x = x + lax.ppermute(x, "tensor", perm)
        step *= 2
    return x


def scatter_kernel(count, rows, part_ref, recv_ref, send_sems, recv_sems):
    me = lax.axis_index("tensor")
    pool_me = lax.axis_index("pool")
    barrier = pltpu.get_barrier_semaphore()
    for d in range(1, count):
        other = lax.rem(me + d, count)
        pl.semaphore_signal(
            barrier, 1, device_id=(pool_me, other), device_id_type=pl.DeviceIdType.MESH
        )
    pl.semaphore_wait(barrier, count - 1)
    copies = []
    for d in range(1, count):
        target = lax.rem(me + d, count)
        start = pl.multiple_of(target * rows, rows)
        copy = pltpu.make_async_remote_copy(
            src_ref=part_ref.at[:, pl.ds(start, rows), :],
            dst_ref=recv_ref.at[d - 1],
            send_sem=send_sems.at[d - 1],
            recv_sem=recv_sems.at[d - 1],
            device_id=(pool_me, target),
            device_id_type=pl.DeviceIdType.MESH,
        )
        copy.start()
        copies.append(copy)
    for copy in copies:
        copy.wait()


def scatter_rows(partial_value, count, rows):
    chunks, _, width = partial_value.shape
    return pl.pallas_call(
        functools.partial(scatter_kernel, count, rows),
        out_shape=jax.ShapeDtypeStruct((count - 1, chunks, rows, width), partial_value.dtype),
        in_specs=[pl.BlockSpec(memory_space=pl.ANY)],
        out_specs=pl.BlockSpec(memory_space=pl.ANY),
        scratch_shapes=[
            pltpu.SemaphoreType.DMA((count - 1,)),
            pltpu.SemaphoreType.DMA((count - 1,)),
        ],
        compiler_params=pltpu.CompilerParams(collective_id=0, has_side_effects=True),
    )(partial_value)


def shards(hidden, down_weight, adapter_shrink, adapter_expand, block_adapter, block_rows):
    input_rows, feat = hidden.shape
    block_count = block_adapter.shape[0]
    pool_count = lax.axis_size("pool")
    tensor_pos = lax.axis_index("tensor")
    tensor_count = lax.axis_size("tensor")
    own_rows = input_rows // tensor_count
    held, _, rank = adapter_shrink.shape
    column_span = adapter_expand.shape[1]
    width = down_weight.shape[1]
    half = width // 2

    w_first = lax.all_gather(down_weight[:, :half], "pool", axis=0, tiled=False)
    part_first = jnp.einsum(
        "if,pfj->pij", hidden, w_first, preferred_element_type=jnp.float32
    ).astype(jnp.bfloat16)
    received = scatter_rows(part_first, tensor_count, own_rows)
    own = lax.dynamic_slice_in_dim(part_first, tensor_pos * own_rows, own_rows, axis=1)
    sum_first = own.astype(jnp.float32) + jnp.sum(received.astype(jnp.float32), axis=0)

    shrink_rows = held * feat * rank // half
    expand_rows = held * column_span * rank // half
    pack = jnp.concatenate(
        [
            down_weight[:, half:],
            adapter_shrink.reshape(shrink_rows, half),
            adapter_expand.reshape(expand_rows, half),
        ],
        axis=0,
    )
    gathered = lax.all_gather(pack, "pool", axis=0, tiled=False)
    w_second = gathered[:, :feat, :]
    shrink_all = gathered[:, feat:feat + shrink_rows, :].reshape(
        pool_count * held, shrink_rows // held, half
    )
    expand_all = gathered[:, feat + shrink_rows:, :].reshape(
        pool_count * held, expand_rows // held, half
    )
    part_second = jnp.einsum(
        "if,pfj->pij", hidden, w_second, preferred_element_type=jnp.float32
    ).astype(jnp.bfloat16)
    sum_second = lax.psum_scatter(part_second, "tensor", scatter_dimension=1, tiled=True)

    first = jnp.take(shrink_all, block_adapter, axis=0).reshape(block_count, feat, rank)
    second = jnp.take(expand_all, block_adapter, axis=0).reshape(block_count, column_span, rank)
    blocks = hidden.reshape(block_count, BLOCK, feat)
    shrink = jnp.einsum("bnf,bfr->bnr", blocks, first, preferred_element_type=jnp.float32)
    summed_shrink = tensor_allsum(shrink, tensor_count).astype(jnp.bfloat16)
    enlarged_rows = jnp.einsum(
        "bnr,bcr->bnc", summed_shrink, second, preferred_element_type=jnp.float32
    )
    delta = (adapter_scale_factor * enlarged_rows).astype(jnp.bfloat16).reshape(input_rows, column_span)
    delta_mine = lax.all_to_all(delta, "tensor", split_axis=0, concat_axis=1, tiled=True)

    total = jnp.concatenate([sum_first, sum_second.astype(jnp.float32)], axis=2)
    total = jnp.transpose(total, (1, 0, 2)).reshape(own_rows, pool_count * width)
    total = total + delta_mine.astype(jnp.float32)

    row_ids = tensor_pos * own_rows + jnp.arange(own_rows, dtype=jnp.int32)
    owning = (row_ids // BLOCK)[:, None] == jnp.arange(block_count, dtype=jnp.int32)[None, :]
    lengths = jnp.sum(jnp.where(owning, block_rows[None, :], 0), axis=1)
    valid = row_ids % BLOCK < lengths
    return jnp.where(valid[:, None], total, 0.0).astype(jnp.bfloat16)


def solution(mesh):
    in_specs = (
        P("pool", "tensor"),
        P("tensor", "pool"),
        P("pool", "tensor", None),
        P("pool", "tensor", None),
        P("pool"),
        P("pool"),
    )
    out_specs = P(("pool", "tensor"), None)
    return jax.shard_map(shards, mesh=mesh, in_specs=in_specs, out_specs=out_specs, check_vma=False)
```

```python
import functools

import jax
import jax.numpy as jnp
from jax import lax
from jax.experimental import pallas as pl
from jax.experimental.pallas import tpu as pltpu
from jax.sharding import PartitionSpec as P

BLOCK = 128


adapter_scale_factor = 0.5


def tensor_allsum(x, count):
    step = 1
    while step < count:
        perm = [(i, i ^ step) for i in range(count)]
        x = x + lax.ppermute(x, "tensor", perm)
        step *= 2
    return x


def scatter_kernel(count, rows, part_ref, recv_ref, send_sems, recv_sems):
    me = lax.axis_index("tensor")
    pool_me = lax.axis_index("pool")
    barrier = pltpu.get_barrier_semaphore()
    for d in range(1, count):
        other = lax.rem(me + d, count)
        pl.semaphore_signal(
            barrier, 1, device_id=(pool_me, other), device_id_type=pl.DeviceIdType.MESH
        )
    pl.semaphore_wait(barrier, count - 1)
    copies = []
    for d in range(1, count):
        target = lax.rem(me + d, count)
        start = pl.multiple_of(target * rows, rows)
        copy = pltpu.make_async_remote_copy(
            src_ref=part_ref.at[:, pl.ds(start, rows), :],
            dst_ref=recv_ref.at[d - 1],
            send_sem=send_sems.at[d - 1],
            recv_sem=recv_sems.at[d - 1],
            device_id=(pool_me, target),
            device_id_type=pl.DeviceIdType.MESH,
        )
        copy.start()
        copies.append(copy)
    for copy in copies:
        copy.wait()


def scatter_rows(partial_value, count, rows):
    chunks, _, width = partial_value.shape
    return pl.pallas_call(
        functools.partial(scatter_kernel, count, rows),
        out_shape=jax.ShapeDtypeStruct((count - 1, chunks, rows, width), partial_value.dtype),
        in_specs=[pl.BlockSpec(memory_space=pl.ANY)],
        out_specs=pl.BlockSpec(memory_space=pl.ANY),
        scratch_shapes=[
            pltpu.SemaphoreType.DMA((count - 1,)),
            pltpu.SemaphoreType.DMA((count - 1,)),
        ],
        compiler_params=pltpu.CompilerParams(collective_id=0, has_side_effects=True),
    )(partial_value)


def tensor_shift(x, side, step, along_y):
    perm = []
    for yy in range(side):
        for xx in range(side):
            if along_y:
                perm.append((yy * side + xx, ((yy + step) % side) * side + xx))
            else:
                perm.append((yy * side + xx, yy * side + (xx + step) % side))
    return lax.ppermute(x, "tensor", perm)


def shards(hidden, down_weight, adapter_shrink, adapter_expand, block_adapter, block_rows):
    input_rows, feat = hidden.shape
    block_count = block_adapter.shape[0]
    pool_count = lax.axis_size("pool")
    tensor_pos = lax.axis_index("tensor")
    tensor_count = lax.axis_size("tensor")
    side = 4
    quarter = pool_count // side
    my_y = tensor_pos // side
    my_x = tensor_pos % side
    own_rows = input_rows // tensor_count
    held, _, rank = adapter_shrink.shape
    column_span = adapter_expand.shape[1]
    width = down_weight.shape[1]

    pairs = []
    for p1 in range(pool_count):
        for y1 in range(side):
            for x1 in range(side):
                p2 = (p1 % quarter) * side + y1
                y2 = p1 // quarter
                pairs.append((p1 * tensor_count + y1 * side + x1, p2 * tensor_count + y2 * side + x1))
    moved = lax.ppermute(down_weight, ("pool", "tensor"), pairs)

    shrink_rows = held * feat * rank // width
    expand_rows = held * column_span * rank // width
    pack = jnp.concatenate(
        [
            moved,
            adapter_shrink.reshape(shrink_rows, width),
            adapter_expand.reshape(expand_rows, width),
        ],
        axis=0,
    )
    gathered = lax.all_gather(pack, "pool", axis=0, tiled=False)
    w_quarter = gathered[:, :feat, :].reshape(quarter, side, feat, width)
    shrink_all = gathered[:, feat:feat + shrink_rows, :].reshape(
        pool_count * held, shrink_rows // held, width
    )
    expand_all = gathered[:, feat + shrink_rows:, :].reshape(
        pool_count * held, expand_rows // held, width
    )

    pieces = [hidden] + [tensor_shift(hidden, side, s, True) for s in range(1, side)]
    by_shift = jnp.stack(pieces, axis=0)
    order = (my_y - jnp.arange(side, dtype=jnp.int32)) % side
    hidden_column = jnp.take(by_shift, order, axis=0)

    first = jnp.take(shrink_all, block_adapter, axis=0).reshape(block_count, feat, rank)
    second = jnp.take(expand_all, block_adapter, axis=0).reshape(block_count, column_span, rank)
    blocks = hidden.reshape(block_count, BLOCK, feat)
    shrink = jnp.einsum("bnf,bfr->bnr", blocks, first, preferred_element_type=jnp.float32)
    summed_shrink = tensor_allsum(shrink, tensor_count).astype(jnp.bfloat16)
    enlarged_rows = jnp.einsum(
        "bnr,bcr->bnc", summed_shrink, second, preferred_element_type=jnp.float32
    )
    delta = (adapter_scale_factor * enlarged_rows).astype(jnp.bfloat16).reshape(input_rows, column_span)

    partial_value = jnp.einsum(
        "yif,ayfj->aij", hidden_column, w_quarter, preferred_element_type=jnp.float32
    )
    chunk_ids = jnp.arange(quarter, dtype=jnp.int32)[:, None, None]
    partial_value = partial_value + jnp.where(
        chunk_ids == my_x, delta.astype(jnp.float32)[None, :, :], 0.0
    )
    partial_value = partial_value.astype(jnp.bfloat16).reshape(
        quarter, side, side, own_rows, width
    )

    total = lax.dynamic_index_in_dim(partial_value, my_x, axis=2, keepdims=False).astype(jnp.float32)
    for s in range(1, side):
        piece = lax.dynamic_index_in_dim(partial_value, (my_x + s) % side, axis=2, keepdims=False)
        total = total + tensor_shift(piece, side, s, False).astype(jnp.float32)
    total = total.astype(jnp.bfloat16)

    got = [lax.dynamic_index_in_dim(total, my_y, axis=1, keepdims=False)]
    for s in range(1, side):
        piece = lax.dynamic_index_in_dim(total, (my_y + s) % side, axis=1, keepdims=False)
        got.append(tensor_shift(piece, side, s, True))
    by_shift = jnp.stack(got, axis=0)
    result = jnp.take(by_shift, order, axis=0)
    result = jnp.transpose(result, (2, 0, 1, 3)).reshape(own_rows, pool_count * width)

    row_ids = tensor_pos * own_rows + jnp.arange(own_rows, dtype=jnp.int32)
    owning = (row_ids // BLOCK)[:, None] == jnp.arange(block_count, dtype=jnp.int32)[None, :]
    lengths = jnp.sum(jnp.where(owning, block_rows[None, :], 0), axis=1)
    valid = row_ids % BLOCK < lengths
    return jnp.where(valid[:, None], result, jnp.zeros_like(result))


def solution(mesh):
    in_specs = (
        P("pool", "tensor"),
        P("tensor", "pool"),
        P("pool", "tensor", None),
        P("pool", "tensor", None),
        P("pool"),
        P("pool"),
    )
    out_specs = P(("pool", "tensor"), None)
    return jax.shard_map(shards, mesh=mesh, in_specs=in_specs, out_specs=out_specs, check_vma=False)
```

```python
import functools

import jax
import jax.numpy as jnp
from jax import lax
from jax.experimental import pallas as pl
from jax.experimental.pallas import tpu as pltpu
from jax.sharding import PartitionSpec as P

BLOCK = 128


adapter_scale_factor = 0.5


def tensor_allsum(x, count):
    step = 1
    while step < count:
        perm = [(i, i ^ step) for i in range(count)]
        x = x + lax.ppermute(x, "tensor", perm)
        step *= 2
    return x


def scatter_kernel(count, rows, part_ref, recv_ref, send_sems, recv_sems):
    me = lax.axis_index("tensor")
    pool_me = lax.axis_index("pool")
    barrier = pltpu.get_barrier_semaphore()
    for d in range(1, count):
        other = lax.rem(me + d, count)
        pl.semaphore_signal(
            barrier, 1, device_id=(pool_me, other), device_id_type=pl.DeviceIdType.MESH
        )
    pl.semaphore_wait(barrier, count - 1)
    copies = []
    for d in range(1, count):
        target = lax.rem(me + d, count)
        start = pl.multiple_of(target * rows, rows)
        copy = pltpu.make_async_remote_copy(
            src_ref=part_ref.at[:, pl.ds(start, rows), :],
            dst_ref=recv_ref.at[d - 1],
            send_sem=send_sems.at[d - 1],
            recv_sem=recv_sems.at[d - 1],
            device_id=(pool_me, target),
            device_id_type=pl.DeviceIdType.MESH,
        )
        copy.start()
        copies.append(copy)
    for copy in copies:
        copy.wait()


def scatter_rows(partial_value, count, rows):
    chunks, _, width = partial_value.shape
    return pl.pallas_call(
        functools.partial(scatter_kernel, count, rows),
        out_shape=jax.ShapeDtypeStruct((count - 1, chunks, rows, width), partial_value.dtype),
        in_specs=[pl.BlockSpec(memory_space=pl.ANY)],
        out_specs=pl.BlockSpec(memory_space=pl.ANY),
        scratch_shapes=[
            pltpu.SemaphoreType.DMA((count - 1,)),
            pltpu.SemaphoreType.DMA((count - 1,)),
        ],
        compiler_params=pltpu.CompilerParams(collective_id=0, has_side_effects=True),
    )(partial_value)


def tensor_shift(x, side, step, along_y):
    perm = []
    for yy in range(side):
        for xx in range(side):
            if along_y:
                perm.append((yy * side + xx, ((yy + step) % side) * side + xx))
            else:
                perm.append((yy * side + xx, yy * side + (xx + step) % side))
    return lax.ppermute(x, "tensor", perm)


def shards(hidden, down_weight, adapter_shrink, adapter_expand, block_adapter, block_rows):
    input_rows, feat = hidden.shape
    block_count = block_adapter.shape[0]
    pool_count = lax.axis_size("pool")
    tensor_pos = lax.axis_index("tensor")
    tensor_count = lax.axis_size("tensor")
    side = 4
    quarter = pool_count // side
    my_y = tensor_pos // side
    my_x = tensor_pos % side
    own_rows = input_rows // tensor_count
    held, _, rank = adapter_shrink.shape
    column_span = adapter_expand.shape[1]
    width = down_weight.shape[1]

    pairs = []
    for p1 in range(pool_count):
        for y1 in range(side):
            for x1 in range(side):
                p2 = (p1 % quarter) * side + y1
                y2 = p1 // quarter
                pairs.append((p1 * tensor_count + y1 * side + x1, p2 * tensor_count + y2 * side + x1))
    moved = lax.ppermute(down_weight, ("pool", "tensor"), pairs)

    shrink_rows = held * feat * rank // width
    expand_rows = held * column_span * rank // width
    pack = jnp.concatenate(
        [
            moved,
            adapter_shrink.reshape(shrink_rows, width),
            adapter_expand.reshape(expand_rows, width),
        ],
        axis=0,
    )
    gathered = lax.all_gather(pack, "pool", axis=0, tiled=False)
    plane_rows = gathered.shape[1]
    w_quarter = gathered.reshape(quarter, side, plane_rows, width)
    shrink_all = gathered[:, feat:feat + shrink_rows, :].reshape(
        pool_count * held, shrink_rows // held, width
    )
    expand_all = gathered[:, feat + shrink_rows:, :].reshape(
        pool_count * held, expand_rows // held, width
    )

    pieces = [hidden] + [tensor_shift(hidden, side, s, True) for s in range(1, side)]
    by_shift = jnp.stack(pieces, axis=0)
    order = (my_y - jnp.arange(side, dtype=jnp.int32)) % side
    hidden_column = jnp.take(by_shift, order, axis=0)
    hidden_column = jnp.pad(hidden_column, ((0, 0), (0, 0), (0, plane_rows - feat)))

    first = jnp.take(shrink_all, block_adapter, axis=0).reshape(block_count, feat, rank)
    second = jnp.take(expand_all, block_adapter, axis=0).reshape(block_count, column_span, rank)
    blocks = hidden.reshape(block_count, BLOCK, feat)
    shrink = jnp.einsum("bnf,bfr->bnr", blocks, first, preferred_element_type=jnp.float32)
    summed_shrink = tensor_allsum(shrink, tensor_count).astype(jnp.bfloat16)
    enlarged_rows = jnp.einsum(
        "bnr,bcr->bnc", summed_shrink, second, preferred_element_type=jnp.float32
    )
    delta = (adapter_scale_factor * enlarged_rows).astype(jnp.bfloat16).reshape(input_rows, column_span)

    partial_value = jnp.einsum(
        "yif,ayfj->aij", hidden_column, w_quarter, preferred_element_type=jnp.float32
    )
    partial_value = partial_value.astype(jnp.bfloat16).reshape(
        quarter, side, side, own_rows, width
    )

    total = lax.dynamic_index_in_dim(partial_value, my_x, axis=2, keepdims=False).astype(jnp.float32)
    for s in range(1, side):
        piece = lax.dynamic_index_in_dim(partial_value, (my_x + s) % side, axis=2, keepdims=False)
        total = total + tensor_shift(piece, side, s, False).astype(jnp.float32)
    delta_rows = delta.reshape(side, side, own_rows, column_span)
    sent = [lax.dynamic_index_in_dim(delta_rows, my_x, axis=1, keepdims=False)]
    for s in range(1, side):
        piece = lax.dynamic_index_in_dim(delta_rows, (my_x + s) % side, axis=1, keepdims=False)
        sent.append(tensor_shift(piece, side, s, False))
    order_x = (my_x - jnp.arange(side, dtype=jnp.int32)) % side
    delta_here = jnp.take(jnp.stack(sent, axis=0), order_x, axis=0)
    total = (total + delta_here.astype(jnp.float32)).astype(jnp.bfloat16)

    got = [lax.dynamic_index_in_dim(total, my_y, axis=1, keepdims=False)]
    for s in range(1, side):
        piece = lax.dynamic_index_in_dim(total, (my_y + s) % side, axis=1, keepdims=False)
        got.append(tensor_shift(piece, side, s, True))
    by_shift = jnp.stack(got, axis=0)
    result = jnp.take(by_shift, order, axis=0)
    result = jnp.transpose(result, (2, 0, 1, 3)).reshape(own_rows, pool_count * width)

    row_ids = tensor_pos * own_rows + jnp.arange(own_rows, dtype=jnp.int32)
    owning = (row_ids // BLOCK)[:, None] == jnp.arange(block_count, dtype=jnp.int32)[None, :]
    lengths = jnp.sum(jnp.where(owning, block_rows[None, :], 0), axis=1)
    valid = row_ids % BLOCK < lengths
    return jnp.where(valid[:, None], result, jnp.zeros_like(result))


def solution(mesh):
    in_specs = (
        P("pool", "tensor"),
        P("tensor", "pool"),
        P("pool", "tensor", None),
        P("pool", "tensor", None),
        P("pool"),
        P("pool"),
    )
    out_specs = P(("pool", "tensor"), None)
    return jax.shard_map(shards, mesh=mesh, in_specs=in_specs, out_specs=out_specs, check_vma=False)
```

```python
import functools

import jax
import jax.numpy as jnp
from jax import lax
from jax.experimental import pallas as pl
from jax.experimental.pallas import tpu as pltpu
from jax.sharding import PartitionSpec as P

BLOCK = 128


adapter_scale_factor = 0.5


def tensor_allsum(x, count):
    step = 1
    while step < count:
        perm = [(i, i ^ step) for i in range(count)]
        x = x + lax.ppermute(x, "tensor", perm)
        step *= 2
    return x


def scatter_kernel(count, rows, part_ref, recv_ref, send_sems, recv_sems):
    me = lax.axis_index("tensor")
    pool_me = lax.axis_index("pool")
    barrier = pltpu.get_barrier_semaphore()
    for d in range(1, count):
        other = lax.rem(me + d, count)
        pl.semaphore_signal(
            barrier, 1, device_id=(pool_me, other), device_id_type=pl.DeviceIdType.MESH
        )
    pl.semaphore_wait(barrier, count - 1)
    copies = []
    for d in range(1, count):
        target = lax.rem(me + d, count)
        start = pl.multiple_of(target * rows, rows)
        copy = pltpu.make_async_remote_copy(
            src_ref=part_ref.at[:, pl.ds(start, rows), :],
            dst_ref=recv_ref.at[d - 1],
            send_sem=send_sems.at[d - 1],
            recv_sem=recv_sems.at[d - 1],
            device_id=(pool_me, target),
            device_id_type=pl.DeviceIdType.MESH,
        )
        copy.start()
        copies.append(copy)
    for copy in copies:
        copy.wait()


def scatter_rows(partial_value, count, rows):
    chunks, _, width = partial_value.shape
    return pl.pallas_call(
        functools.partial(scatter_kernel, count, rows),
        out_shape=jax.ShapeDtypeStruct((count - 1, chunks, rows, width), partial_value.dtype),
        in_specs=[pl.BlockSpec(memory_space=pl.ANY)],
        out_specs=pl.BlockSpec(memory_space=pl.ANY),
        scratch_shapes=[
            pltpu.SemaphoreType.DMA((count - 1,)),
            pltpu.SemaphoreType.DMA((count - 1,)),
        ],
        compiler_params=pltpu.CompilerParams(collective_id=0, has_side_effects=True),
    )(partial_value)


def tensor_shift(x, side, step, along_y):
    perm = []
    for yy in range(side):
        for xx in range(side):
            if along_y:
                perm.append((yy * side + xx, ((yy + step) % side) * side + xx))
            else:
                perm.append((yy * side + xx, yy * side + (xx + step) % side))
    return lax.ppermute(x, "tensor", perm)


def shards(hidden, down_weight, adapter_shrink, adapter_expand, block_adapter, block_rows):
    input_rows, feat = hidden.shape
    block_count = block_adapter.shape[0]
    pool_count = lax.axis_size("pool")
    tensor_pos = lax.axis_index("tensor")
    tensor_count = lax.axis_size("tensor")
    side = 4
    quarter = pool_count // side
    my_y = tensor_pos // side
    my_x = tensor_pos % side
    own_rows = input_rows // tensor_count
    held, _, rank = adapter_shrink.shape
    column_span = adapter_expand.shape[1]
    width = down_weight.shape[1]

    pairs = []
    for p1 in range(pool_count):
        for y1 in range(side):
            for x1 in range(side):
                y2 = p1 % side
                p2 = (p1 // side) * side + (y2 - y1) % side
                pairs.append((p1 * tensor_count + y1 * side + x1, p2 * tensor_count + y2 * side + x1))
    moved = lax.ppermute(down_weight, ("pool", "tensor"), pairs)

    shrink_rows = held * feat * rank // width
    expand_rows = held * column_span * rank // width
    pack = jnp.concatenate(
        [
            moved,
            adapter_shrink.reshape(shrink_rows, width),
            adapter_expand.reshape(expand_rows, width),
        ],
        axis=0,
    )
    gathered = lax.all_gather(pack, "pool", axis=0, tiled=False)
    plane_rows = gathered.shape[1]
    w_quarter = gathered.reshape(quarter, side, plane_rows, width)
    shrink_all = gathered[:, feat:feat + shrink_rows, :].reshape(
        pool_count * held, shrink_rows // held, width
    )
    expand_all = gathered[:, feat + shrink_rows:, :].reshape(
        pool_count * held, expand_rows // held, width
    )

    pieces = [hidden] + [tensor_shift(hidden, side, s, True) for s in range(1, side)]
    hidden_column = jnp.pad(jnp.stack(pieces, axis=0), ((0, 0), (0, 0), (0, plane_rows - feat)))

    first = jnp.take(shrink_all, block_adapter, axis=0).reshape(block_count, feat, rank)
    second = jnp.take(expand_all, block_adapter, axis=0).reshape(block_count, column_span, rank)
    blocks = hidden.reshape(block_count, BLOCK, feat)
    shrink = jnp.einsum("bnf,bfr->bnr", blocks, first, preferred_element_type=jnp.float32)
    summed_shrink = tensor_allsum(shrink, tensor_count).astype(jnp.bfloat16)
    enlarged_rows = jnp.einsum(
        "bnr,bcr->bnc", summed_shrink, second, preferred_element_type=jnp.float32
    )
    delta = (adapter_scale_factor * enlarged_rows).astype(jnp.bfloat16).reshape(input_rows, column_span)

    partial_value = jnp.einsum(
        "sif,asfj->aij", hidden_column, w_quarter, preferred_element_type=jnp.float32
    )
    partial_value = partial_value.astype(jnp.bfloat16).reshape(
        quarter, side, side, own_rows, width
    )

    total = lax.dynamic_index_in_dim(partial_value, my_x, axis=2, keepdims=False).astype(jnp.float32)
    for s in range(1, side):
        piece = lax.dynamic_index_in_dim(partial_value, (my_x + s) % side, axis=2, keepdims=False)
        total = total + tensor_shift(piece, side, s, False).astype(jnp.float32)
    total = total.astype(jnp.bfloat16)

    got = [lax.dynamic_index_in_dim(total, my_y, axis=1, keepdims=False)]
    for s in range(1, side):
        piece = lax.dynamic_index_in_dim(total, (my_y + s) % side, axis=1, keepdims=False)
        got.append(tensor_shift(piece, side, s, True))
    order = (my_y - jnp.arange(side, dtype=jnp.int32)) % side
    result = jnp.take(jnp.stack(got, axis=0), order, axis=0)
    result = jnp.transpose(result, (2, 1, 0, 3)).reshape(own_rows, pool_count * width)
    delta_mine = lax.all_to_all(delta, "tensor", split_axis=0, concat_axis=1, tiled=True)
    result = (result.astype(jnp.float32) + delta_mine.astype(jnp.float32)).astype(jnp.bfloat16)

    row_ids = tensor_pos * own_rows + jnp.arange(own_rows, dtype=jnp.int32)
    owning = (row_ids // BLOCK)[:, None] == jnp.arange(block_count, dtype=jnp.int32)[None, :]
    lengths = jnp.sum(jnp.where(owning, block_rows[None, :], 0), axis=1)
    valid = row_ids % BLOCK < lengths
    return jnp.where(valid[:, None], result, jnp.zeros_like(result))


def solution(mesh):
    in_specs = (
        P("pool", "tensor"),
        P("tensor", "pool"),
        P("pool", "tensor", None),
        P("pool", "tensor", None),
        P("pool"),
        P("pool"),
    )
    out_specs = P(("pool", "tensor"), None)
    return jax.shard_map(shards, mesh=mesh, in_specs=in_specs, out_specs=out_specs, check_vma=False)
```

```python
import functools

import jax
import jax.numpy as jnp
from jax import lax
from jax.experimental import pallas as pl
from jax.experimental.pallas import tpu as pltpu
from jax.sharding import PartitionSpec as P

BLOCK = 128


adapter_scale_factor = 0.5


def tensor_allsum(x, count):
    step = 1
    while step < count:
        perm = [(i, i ^ step) for i in range(count)]
        x = x + lax.ppermute(x, "tensor", perm)
        step *= 2
    return x


def x_reduce_kernel(side, part_ref, recv_ref, send_sems, recv_sems):
    me = lax.axis_index("tensor")
    pool_me = lax.axis_index("pool")
    my_y = me // side
    my_x = me % side
    barrier = pltpu.get_barrier_semaphore()
    for s in range(1, side):
        other = my_y * side + lax.rem(my_x + s, side)
        pl.semaphore_signal(
            barrier, 1, device_id=(pool_me, other), device_id_type=pl.DeviceIdType.MESH
        )
    pl.semaphore_wait(barrier, side - 1)
    copies = []
    for s in range(1, side):
        target_x = lax.rem(my_x + s, side)
        copy = pltpu.make_async_remote_copy(
            src_ref=part_ref.at[:, pl.ds(target_x, 1)],
            dst_ref=recv_ref.at[s - 1],
            send_sem=send_sems.at[s - 1],
            recv_sem=recv_sems.at[s - 1],
            device_id=(pool_me, my_y * side + target_x),
            device_id_type=pl.DeviceIdType.MESH,
        )
        copy.start()
        copies.append(copy)
    for copy in copies:
        copy.wait()


def x_reduce_send(partial_value, side):
    groups, _, rows, width = partial_value.shape
    return pl.pallas_call(
        functools.partial(x_reduce_kernel, side),
        out_shape=jax.ShapeDtypeStruct((side - 1, groups, 1, rows, width), partial_value.dtype),
        in_specs=[pl.BlockSpec(memory_space=pl.ANY)],
        out_specs=pl.BlockSpec(memory_space=pl.ANY),
        scratch_shapes=[
            pltpu.SemaphoreType.DMA((side - 1,)),
            pltpu.SemaphoreType.DMA((side - 1,)),
        ],
        compiler_params=pltpu.CompilerParams(collective_id=0, has_side_effects=True),
    )(partial_value)


def tensor_shift(x, side, step, along_y):
    perm = []
    for yy in range(side):
        for xx in range(side):
            if along_y:
                perm.append((yy * side + xx, ((yy + step) % side) * side + xx))
            else:
                perm.append((yy * side + xx, yy * side + (xx + step) % side))
    return lax.ppermute(x, "tensor", perm)


def shards(hidden, down_weight, adapter_shrink, adapter_expand, block_adapter, block_rows):
    input_rows, feat = hidden.shape
    block_count = block_adapter.shape[0]
    pool_count = lax.axis_size("pool")
    tensor_pos = lax.axis_index("tensor")
    tensor_count = lax.axis_size("tensor")
    side = 4
    quarter = pool_count // side
    my_y = tensor_pos // side
    my_x = tensor_pos % side
    own_rows = input_rows // tensor_count
    held, _, rank = adapter_shrink.shape
    column_span = adapter_expand.shape[1]
    width = down_weight.shape[1]

    pairs = []
    for p1 in range(pool_count):
        for y1 in range(side):
            for x1 in range(side):
                y2 = p1 % side
                p2 = (p1 // side) * side + (y2 - y1) % side
                pairs.append((p1 * tensor_count + y1 * side + x1, p2 * tensor_count + y2 * side + x1))
    moved = lax.ppermute(down_weight, ("pool", "tensor"), pairs)

    shrink_rows = held * feat * rank // width
    expand_rows = held * column_span * rank // width
    pack = jnp.concatenate(
        [
            moved,
            adapter_shrink.reshape(shrink_rows, width),
            adapter_expand.reshape(expand_rows, width),
        ],
        axis=0,
    )
    gathered = lax.all_gather(pack, "pool", axis=0, tiled=False)
    plane_rows = gathered.shape[1]
    w_quarter = gathered.reshape(quarter, side, plane_rows, width)
    shrink_all = gathered[:, feat:feat + shrink_rows, :].reshape(
        pool_count * held, shrink_rows // held, width
    )
    expand_all = gathered[:, feat + shrink_rows:, :].reshape(
        pool_count * held, expand_rows // held, width
    )

    pieces = [hidden] + [tensor_shift(hidden, side, s, True) for s in range(1, side)]
    hidden_column = jnp.pad(jnp.stack(pieces, axis=0), ((0, 0), (0, 0), (0, plane_rows - feat)))

    first = jnp.take(shrink_all, block_adapter, axis=0).reshape(block_count, feat, rank)
    second = jnp.take(expand_all, block_adapter, axis=0).reshape(block_count, column_span, rank)
    blocks = hidden.reshape(block_count, BLOCK, feat)
    shrink = jnp.einsum("bnf,bfr->bnr", blocks, first, preferred_element_type=jnp.float32)
    summed_shrink = tensor_allsum(shrink, tensor_count).astype(jnp.bfloat16)
    enlarged_rows = jnp.einsum(
        "bnr,bcr->bnc", summed_shrink, second, preferred_element_type=jnp.float32
    )
    delta = (adapter_scale_factor * enlarged_rows).astype(jnp.bfloat16).reshape(input_rows, column_span)

    partial_value = jnp.einsum(
        "sif,asfj->aij", hidden_column, w_quarter, preferred_element_type=jnp.float32
    )
    partial_value = partial_value.astype(jnp.bfloat16).reshape(
        quarter * side, side, own_rows, width
    )

    received = x_reduce_send(partial_value, side)
    total = lax.dynamic_index_in_dim(partial_value, my_x, axis=1, keepdims=False).astype(jnp.float32)
    total = total + jnp.sum(received[:, :, 0].astype(jnp.float32), axis=0)
    total = total.astype(jnp.bfloat16).reshape(quarter, side, own_rows, width)

    got = [lax.dynamic_index_in_dim(total, my_y, axis=1, keepdims=False)]
    for s in range(1, side):
        piece = lax.dynamic_index_in_dim(total, (my_y + s) % side, axis=1, keepdims=False)
        got.append(tensor_shift(piece, side, s, True))
    order = (my_y - jnp.arange(side, dtype=jnp.int32)) % side
    result = jnp.take(jnp.stack(got, axis=0), order, axis=0)
    result = jnp.transpose(result, (2, 1, 0, 3)).reshape(own_rows, pool_count * width)
    delta_mine = lax.all_to_all(delta, "tensor", split_axis=0, concat_axis=1, tiled=True)
    result = (result.astype(jnp.float32) + delta_mine.astype(jnp.float32)).astype(jnp.bfloat16)

    row_ids = tensor_pos * own_rows + jnp.arange(own_rows, dtype=jnp.int32)
    owning = (row_ids // BLOCK)[:, None] == jnp.arange(block_count, dtype=jnp.int32)[None, :]
    lengths = jnp.sum(jnp.where(owning, block_rows[None, :], 0), axis=1)
    valid = row_ids % BLOCK < lengths
    return jnp.where(valid[:, None], result, jnp.zeros_like(result))


def solution(mesh):
    in_specs = (
        P("pool", "tensor"),
        P("tensor", "pool"),
        P("pool", "tensor", None),
        P("pool", "tensor", None),
        P("pool"),
        P("pool"),
    )
    out_specs = P(("pool", "tensor"), None)
    return jax.shard_map(shards, mesh=mesh, in_specs=in_specs, out_specs=out_specs, check_vma=False)
```

```python
import functools

import jax
import jax.numpy as jnp
from jax import lax
from jax.experimental import pallas as pl
from jax.experimental.pallas import tpu as pltpu
from jax.sharding import PartitionSpec as P

BLOCK = 128


adapter_scale_factor = 0.5


def tensor_shift(x, side, step, along_y):
    perm = []
    for yy in range(side):
        for xx in range(side):
            if along_y:
                perm.append((yy * side + xx, ((yy + step) % side) * side + xx))
            else:
                perm.append((yy * side + xx, yy * side + (xx + step) % side))
    return lax.ppermute(x, "tensor", perm)


def tensor_allsum(x, side):
    for along_y in (False, True):
        x = x + sum(tensor_shift(x, side, s, along_y) for s in range(1, side))
    return x


def y_reduce_kernel(side, part_ref, recv_ref, send_sems, recv_sems):
    me = lax.axis_index("tensor")
    pool_me = lax.axis_index("pool")
    my_y = me // side
    my_x = me % side
    barrier = pltpu.get_barrier_semaphore()
    for s in range(1, side):
        other = lax.rem(my_y + s, side) * side + my_x
        pl.semaphore_signal(
            barrier, 1, device_id=(pool_me, other), device_id_type=pl.DeviceIdType.MESH
        )
    pl.semaphore_wait(barrier, side - 1)
    copies = []
    for s in range(1, side):
        target_y = lax.rem(my_y + s, side)
        copy = pltpu.make_async_remote_copy(
            src_ref=part_ref.at[:, pl.ds(target_y, 1)],
            dst_ref=recv_ref.at[s - 1],
            send_sem=send_sems.at[s - 1],
            recv_sem=recv_sems.at[s - 1],
            device_id=(pool_me, target_y * side + my_x),
            device_id_type=pl.DeviceIdType.MESH,
        )
        copy.start()
        copies.append(copy)
    for copy in copies:
        copy.wait()


def y_reduce_send(partial_value, side):
    groups, _, rows, width = partial_value.shape
    return pl.pallas_call(
        functools.partial(y_reduce_kernel, side),
        out_shape=jax.ShapeDtypeStruct((side - 1, groups, 1, rows, width), partial_value.dtype),
        in_specs=[pl.BlockSpec(memory_space=pl.ANY)],
        out_specs=pl.BlockSpec(memory_space=pl.ANY),
        scratch_shapes=[
            pltpu.SemaphoreType.DMA((side - 1,)),
            pltpu.SemaphoreType.DMA((side - 1,)),
        ],
        compiler_params=pltpu.CompilerParams(collective_id=0, has_side_effects=True),
    )(partial_value)


def shards(hidden, down_weight, adapter_shrink, adapter_expand, block_adapter, block_rows):
    input_rows, feat = hidden.shape
    block_count = block_adapter.shape[0]
    pool_count = lax.axis_size("pool")
    tensor_pos = lax.axis_index("tensor")
    tensor_count = lax.axis_size("tensor")
    side = 4
    quarter = pool_count // side
    my_y = tensor_pos // side
    my_x = tensor_pos % side
    own_rows = input_rows // tensor_count
    held, _, rank = adapter_shrink.shape
    column_span = adapter_expand.shape[1]
    width = down_weight.shape[1]

    pairs = []
    for p1 in range(pool_count):
        for y1 in range(side):
            for x1 in range(side):
                x2 = p1 % side
                p2 = (p1 // side) * side + (x2 - x1) % side
                pairs.append((p1 * tensor_count + y1 * side + x1, p2 * tensor_count + y1 * side + x2))
    moved = lax.ppermute(down_weight, ("pool", "tensor"), pairs)

    shrink_rows = held * feat * rank // width
    expand_rows = held * column_span * rank // width
    pack = jnp.concatenate(
        [
            moved,
            adapter_shrink.reshape(shrink_rows, width),
            adapter_expand.reshape(expand_rows, width),
        ],
        axis=0,
    )
    gathered = lax.all_gather(pack, "pool", axis=0, tiled=False)
    plane_rows = gathered.shape[1]
    w_quarter = gathered.reshape(quarter, side, plane_rows, width)
    shrink_all = gathered[:, feat:feat + shrink_rows, :].reshape(
        pool_count * held, shrink_rows // held, width
    )
    expand_all = gathered[:, feat + shrink_rows:, :].reshape(
        pool_count * held, expand_rows // held, width
    )

    pieces = [hidden] + [tensor_shift(hidden, side, s, False) for s in range(1, side)]
    hidden_column = jnp.pad(jnp.stack(pieces, axis=0), ((0, 0), (0, 0), (0, plane_rows - feat)))

    first = jnp.take(shrink_all, block_adapter, axis=0).reshape(block_count, feat, rank)
    second = jnp.take(expand_all, block_adapter, axis=0).reshape(block_count, column_span, rank)
    blocks = hidden.reshape(block_count, BLOCK, feat)
    shrink = jnp.einsum("bnf,bfr->bnr", blocks, first, preferred_element_type=jnp.float32)
    summed_shrink = tensor_allsum(shrink, side).astype(jnp.bfloat16)
    enlarged_rows = jnp.einsum(
        "bnr,bcr->bnc", summed_shrink, second, preferred_element_type=jnp.float32
    )
    delta = (adapter_scale_factor * enlarged_rows).astype(jnp.bfloat16).reshape(input_rows, column_span)

    partial_value = jnp.einsum(
        "sif,asfj->aij", hidden_column, w_quarter, preferred_element_type=jnp.float32
    )
    chunk_ids = jnp.arange(quarter, dtype=jnp.int32)[:, None, None]
    partial_value = partial_value + jnp.where(
        chunk_ids == my_y, delta.astype(jnp.float32)[None, :, :], 0.0
    )
    partial_value = partial_value.astype(jnp.bfloat16).reshape(
        quarter, side, side, own_rows, width
    )
    partial_value = jnp.transpose(partial_value, (0, 2, 1, 3, 4)).reshape(
        quarter * side, side, own_rows, width
    )

    received = y_reduce_send(partial_value, side)
    total = lax.dynamic_index_in_dim(partial_value, my_y, axis=1, keepdims=False).astype(jnp.float32)
    total = total + jnp.sum(received[:, :, 0].astype(jnp.float32), axis=0)
    total = total.astype(jnp.bfloat16).reshape(quarter, side, own_rows, width)

    got = [lax.dynamic_index_in_dim(total, my_x, axis=1, keepdims=False)]
    for s in range(1, side):
        piece = lax.dynamic_index_in_dim(total, (my_x + s) % side, axis=1, keepdims=False)
        got.append(tensor_shift(piece, side, s, False))
    order = (my_x - jnp.arange(side, dtype=jnp.int32)) % side
    result = jnp.take(jnp.stack(got, axis=0), order, axis=0)
    result = jnp.transpose(result, (2, 1, 0, 3)).reshape(own_rows, pool_count * width)

    row_ids = tensor_pos * own_rows + jnp.arange(own_rows, dtype=jnp.int32)
    owning = (row_ids // BLOCK)[:, None] == jnp.arange(block_count, dtype=jnp.int32)[None, :]
    lengths = jnp.sum(jnp.where(owning, block_rows[None, :], 0), axis=1)
    valid = row_ids % BLOCK < lengths
    return jnp.where(valid[:, None], result, jnp.zeros_like(result))


def solution(mesh):
    in_specs = (
        P("pool", "tensor"),
        P("tensor", "pool"),
        P("pool", "tensor", None),
        P("pool", "tensor", None),
        P("pool"),
        P("pool"),
    )
    out_specs = P(("pool", "tensor"), None)
    return jax.shard_map(shards, mesh=mesh, in_specs=in_specs, out_specs=out_specs, check_vma=False)
```

```python
import functools

import jax
import jax.numpy as jnp
from jax import lax
from jax.experimental import pallas as pl
from jax.experimental.pallas import tpu as pltpu
from jax.sharding import PartitionSpec as P

BLOCK = 128


adapter_scale_factor = 0.5


def tensor_shift(x, side, step, along_y):
    perm = []
    for yy in range(side):
        for xx in range(side):
            if along_y:
                perm.append((yy * side + xx, ((yy + step) % side) * side + xx))
            else:
                perm.append((yy * side + xx, yy * side + (xx + step) % side))
    return lax.ppermute(x, "tensor", perm)


def tensor_allsum(x, side):
    for along_y in (False, True):
        x = x + sum(tensor_shift(x, side, s, along_y) for s in range(1, side))
    return x


def y_reduce_kernel(side, part_ref, recv_ref, send_sems, recv_sems):
    me = lax.axis_index("tensor")
    pool_me = lax.axis_index("pool")
    my_y = me // side
    my_x = me % side
    barrier = pltpu.get_barrier_semaphore()
    for s in range(1, side):
        other = lax.rem(my_y + s, side) * side + my_x
        pl.semaphore_signal(
            barrier, 1, device_id=(pool_me, other), device_id_type=pl.DeviceIdType.MESH
        )
    pl.semaphore_wait(barrier, side - 1)
    copies = []
    for s in range(1, side):
        target_y = lax.rem(my_y + s, side)
        copy = pltpu.make_async_remote_copy(
            src_ref=part_ref.at[:, pl.ds(target_y, 1)],
            dst_ref=recv_ref.at[s - 1],
            send_sem=send_sems.at[s - 1],
            recv_sem=recv_sems.at[s - 1],
            device_id=(pool_me, target_y * side + my_x),
            device_id_type=pl.DeviceIdType.MESH,
        )
        copy.start()
        copies.append(copy)
    for copy in copies:
        copy.wait()


def y_reduce_send(partial_value, side):
    groups, _, rows, width = partial_value.shape
    return pl.pallas_call(
        functools.partial(y_reduce_kernel, side),
        out_shape=jax.ShapeDtypeStruct((side - 1, groups, 1, rows, width), partial_value.dtype),
        in_specs=[pl.BlockSpec(memory_space=pl.ANY)],
        out_specs=pl.BlockSpec(memory_space=pl.ANY),
        scratch_shapes=[
            pltpu.SemaphoreType.DMA((side - 1,)),
            pltpu.SemaphoreType.DMA((side - 1,)),
        ],
        compiler_params=pltpu.CompilerParams(collective_id=0, has_side_effects=True),
    )(partial_value)


def shards(hidden, down_weight, adapter_shrink, adapter_expand, block_adapter, block_rows):
    input_rows, feat = hidden.shape
    block_count = block_adapter.shape[0]
    pool_count = lax.axis_size("pool")
    tensor_pos = lax.axis_index("tensor")
    tensor_count = lax.axis_size("tensor")
    side = 4
    quarter = pool_count // side
    my_y = tensor_pos // side
    my_x = tensor_pos % side
    own_rows = input_rows // tensor_count
    held, _, rank = adapter_shrink.shape
    column_span = adapter_expand.shape[1]
    width = down_weight.shape[1]

    pairs = []
    for p1 in range(pool_count):
        for y1 in range(side):
            for x1 in range(side):
                x2 = p1 % side
                p2 = (p1 // side) * side + (x2 - x1) % side
                pairs.append((p1 * tensor_count + y1 * side + x1, p2 * tensor_count + y1 * side + x2))
    moved = lax.ppermute(down_weight, ("pool", "tensor"), pairs)

    shrink_rows = held * feat * rank // width
    expand_rows = held * column_span * rank // width
    pack = jnp.concatenate(
        [
            moved,
            adapter_shrink.reshape(shrink_rows, width),
            adapter_expand.reshape(expand_rows, width),
        ],
        axis=0,
    )
    pieces = [hidden] + [tensor_shift(hidden, side, s, False) for s in range(1, side)]
    pack, pieces = lax.optimization_barrier((pack, pieces))
    gathered = lax.all_gather(pack, "pool", axis=0, tiled=False)
    plane_rows = gathered.shape[1]
    w_quarter = gathered.reshape(quarter, side, plane_rows, width)
    shrink_all = gathered[:, feat:feat + shrink_rows, :].reshape(
        pool_count * held, shrink_rows // held, width
    )
    expand_all = gathered[:, feat + shrink_rows:, :].reshape(
        pool_count * held, expand_rows // held, width
    )

    hidden_column = jnp.pad(jnp.stack(pieces, axis=0), ((0, 0), (0, 0), (0, plane_rows - feat)))

    first = jnp.take(shrink_all, block_adapter, axis=0).reshape(block_count, feat, rank)
    second = jnp.take(expand_all, block_adapter, axis=0).reshape(block_count, column_span, rank)
    blocks = hidden.reshape(block_count, BLOCK, feat)
    shrink = jnp.einsum("bnf,bfr->bnr", blocks, first, preferred_element_type=jnp.float32)
    summed_shrink = tensor_allsum(shrink, side).astype(jnp.bfloat16)
    enlarged_rows = jnp.einsum(
        "bnr,bcr->bnc", summed_shrink, second, preferred_element_type=jnp.float32
    )
    delta = (adapter_scale_factor * enlarged_rows).astype(jnp.bfloat16).reshape(input_rows, column_span)

    partial_value = jnp.einsum(
        "sif,asfj->aij", hidden_column, w_quarter, preferred_element_type=jnp.float32
    )
    chunk_ids = jnp.arange(quarter, dtype=jnp.int32)[:, None, None]
    partial_value = partial_value + jnp.where(
        chunk_ids == my_y, delta.astype(jnp.float32)[None, :, :], 0.0
    )
    partial_value = partial_value.astype(jnp.bfloat16).reshape(
        quarter, side, side, own_rows, width
    )
    partial_value = jnp.transpose(partial_value, (0, 2, 1, 3, 4)).reshape(
        quarter * side, side, own_rows, width
    )

    received = y_reduce_send(partial_value, side)
    total = lax.dynamic_index_in_dim(partial_value, my_y, axis=1, keepdims=False).astype(jnp.float32)
    total = total + jnp.sum(received[:, :, 0].astype(jnp.float32), axis=0)
    total = total.astype(jnp.bfloat16).reshape(quarter, side, own_rows, width)

    got = [lax.dynamic_index_in_dim(total, my_x, axis=1, keepdims=False)]
    for s in range(1, side):
        piece = lax.dynamic_index_in_dim(total, (my_x + s) % side, axis=1, keepdims=False)
        got.append(tensor_shift(piece, side, s, False))
    order = (my_x - jnp.arange(side, dtype=jnp.int32)) % side
    result = jnp.take(jnp.stack(got, axis=0), order, axis=0)
    result = jnp.transpose(result, (2, 1, 0, 3)).reshape(own_rows, pool_count * width)

    row_ids = tensor_pos * own_rows + jnp.arange(own_rows, dtype=jnp.int32)
    owning = (row_ids // BLOCK)[:, None] == jnp.arange(block_count, dtype=jnp.int32)[None, :]
    lengths = jnp.sum(jnp.where(owning, block_rows[None, :], 0), axis=1)
    valid = row_ids % BLOCK < lengths
    return jnp.where(valid[:, None], result, jnp.zeros_like(result))


def solution(mesh):
    in_specs = (
        P("pool", "tensor"),
        P("tensor", "pool"),
        P("pool", "tensor", None),
        P("pool", "tensor", None),
        P("pool"),
        P("pool"),
    )
    out_specs = P(("pool", "tensor"), None)
    return jax.shard_map(shards, mesh=mesh, in_specs=in_specs, out_specs=out_specs, check_vma=False)
```

```python
import functools

import jax
import jax.numpy as jnp
from jax import lax
from jax.experimental import pallas as pl
from jax.experimental.pallas import tpu as pltpu
from jax.sharding import PartitionSpec as P

BLOCK = 128


adapter_scale_factor = 0.5


def tensor_shift(x, side, step, along_y):
    perm = []
    for yy in range(side):
        for xx in range(side):
            if along_y:
                perm.append((yy * side + xx, ((yy + step) % side) * side + xx))
            else:
                perm.append((yy * side + xx, yy * side + (xx + step) % side))
    return lax.ppermute(x, "tensor", perm)


def tensor_allsum(x, side):
    for along_y in (False, True):
        x = x + sum(tensor_shift(x, side, s, along_y) for s in range(1, side))
    return x


def scatter_kernel(count, rows, part_ref, recv_ref, send_sems, recv_sems):
    me = lax.axis_index("tensor")
    pool_me = lax.axis_index("pool")
    barrier = pltpu.get_barrier_semaphore()
    for d in range(1, count):
        other = lax.rem(me + d, count)
        pl.semaphore_signal(
            barrier, 1, device_id=(pool_me, other), device_id_type=pl.DeviceIdType.MESH
        )
    pl.semaphore_wait(barrier, count - 1)
    copies = []
    for d in range(1, count):
        target = lax.rem(me + d, count)
        start = pl.multiple_of(target * rows, rows)
        copy = pltpu.make_async_remote_copy(
            src_ref=part_ref.at[:, pl.ds(start, rows), :],
            dst_ref=recv_ref.at[d - 1],
            send_sem=send_sems.at[d - 1],
            recv_sem=recv_sems.at[d - 1],
            device_id=(pool_me, target),
            device_id_type=pl.DeviceIdType.MESH,
        )
        copy.start()
        copies.append(copy)
    for copy in copies:
        copy.wait()


def scatter_rows(partial_value, count, rows):
    chunks, _, width = partial_value.shape
    return pl.pallas_call(
        functools.partial(scatter_kernel, count, rows),
        out_shape=jax.ShapeDtypeStruct((count - 1, chunks, rows, width), partial_value.dtype),
        in_specs=[pl.BlockSpec(memory_space=pl.ANY)],
        out_specs=pl.BlockSpec(memory_space=pl.ANY),
        scratch_shapes=[
            pltpu.SemaphoreType.DMA((count - 1,)),
            pltpu.SemaphoreType.DMA((count - 1,)),
        ],
        compiler_params=pltpu.CompilerParams(collective_id=0, has_side_effects=True),
    )(partial_value)


def shards(hidden, down_weight, adapter_shrink, adapter_expand, block_adapter, block_rows):
    input_rows, feat = hidden.shape
    block_count = block_adapter.shape[0]
    pool_count = lax.axis_size("pool")
    tensor_pos = lax.axis_index("tensor")
    tensor_count = lax.axis_size("tensor")
    side = 4
    quarter = pool_count // side
    my_y = tensor_pos // side
    my_x = tensor_pos % side
    own_rows = input_rows // tensor_count
    held, _, rank = adapter_shrink.shape
    column_span = adapter_expand.shape[1]
    width = down_weight.shape[1]

    pairs = []
    for p1 in range(pool_count):
        for y1 in range(side):
            for x1 in range(side):
                y2 = p1 % side
                p2 = (p1 // side) * side + (y2 - y1) % side
                pairs.append((p1 * tensor_count + y1 * side + x1, p2 * tensor_count + y2 * side + x1))
    moved = lax.ppermute(down_weight, ("pool", "tensor"), pairs)

    shrink_rows = held * feat * rank // width
    expand_rows = held * column_span * rank // width
    pack = jnp.concatenate(
        [
            moved,
            adapter_shrink.reshape(shrink_rows, width),
            adapter_expand.reshape(expand_rows, width),
        ],
        axis=0,
    )
    gathered = lax.all_gather(pack, "pool", axis=0, tiled=False)
    plane_rows = gathered.shape[1]
    w_quarter = gathered.reshape(quarter, side, plane_rows, width)
    shrink_all = gathered[:, feat:feat + shrink_rows, :].reshape(
        pool_count * held, shrink_rows // held, width
    )
    expand_all = gathered[:, feat + shrink_rows:, :].reshape(
        pool_count * held, expand_rows // held, width
    )

    pieces = [hidden] + [tensor_shift(hidden, side, s, True) for s in range(1, side)]
    hidden_column = jnp.stack(pieces, axis=0).reshape(side, side, side, own_rows, feat)
    hidden_column = jnp.transpose(hidden_column, (2, 0, 1, 3, 4)).reshape(
        side, side, side * own_rows, feat
    )
    hidden_column = jnp.pad(hidden_column, ((0, 0), (0, 0), (0, 0), (0, plane_rows - feat)))

    first = jnp.take(shrink_all, block_adapter, axis=0).reshape(block_count, feat, rank)
    second = jnp.take(expand_all, block_adapter, axis=0).reshape(block_count, column_span, rank)
    blocks = hidden.reshape(block_count, BLOCK, feat)
    shrink = jnp.einsum("bnf,bfr->bnr", blocks, first, preferred_element_type=jnp.float32)
    summed_shrink = tensor_allsum(shrink, side).astype(jnp.bfloat16)
    enlarged_rows = jnp.einsum(
        "bnr,bcr->bnc", summed_shrink, second, preferred_element_type=jnp.float32
    )
    delta = (adapter_scale_factor * enlarged_rows).astype(jnp.bfloat16).reshape(input_rows, column_span)

    def rows_for(owner_x):
        rows = lax.dynamic_index_in_dim(hidden_column, owner_x, axis=0, keepdims=False)
        piece = jnp.einsum("sif,asfj->aij", rows, w_quarter, preferred_element_type=jnp.float32)
        return piece.astype(jnp.bfloat16).reshape(quarter, side, own_rows, width)

    total = None
    for s in range(1, side):
        arrived = tensor_shift(rows_for((my_x + s) % side), side, s, False).astype(jnp.float32)
        total = arrived if total is None else total + arrived
    total = (total + rows_for(my_x).astype(jnp.float32)).astype(jnp.bfloat16)

    got = [lax.dynamic_index_in_dim(total, my_y, axis=1, keepdims=False)]
    for s in range(1, side):
        piece = lax.dynamic_index_in_dim(total, (my_y + s) % side, axis=1, keepdims=False)
        got.append(tensor_shift(piece, side, s, True))
    order = (my_y - jnp.arange(side, dtype=jnp.int32)) % side
    result = jnp.take(jnp.stack(got, axis=0), order, axis=0)
    result = jnp.transpose(result, (2, 1, 0, 3)).reshape(own_rows, pool_count * width)
    delta_mine = lax.all_to_all(delta, "tensor", split_axis=0, concat_axis=1, tiled=True)
    result = (result.astype(jnp.float32) + delta_mine.astype(jnp.float32)).astype(jnp.bfloat16)

    row_ids = tensor_pos * own_rows + jnp.arange(own_rows, dtype=jnp.int32)
    owning = (row_ids // BLOCK)[:, None] == jnp.arange(block_count, dtype=jnp.int32)[None, :]
    lengths = jnp.sum(jnp.where(owning, block_rows[None, :], 0), axis=1)
    valid = row_ids % BLOCK < lengths
    return jnp.where(valid[:, None], result, jnp.zeros_like(result))


def solution(mesh):
    in_specs = (
        P("pool", "tensor"),
        P("tensor", "pool"),
        P("pool", "tensor", None),
        P("pool", "tensor", None),
        P("pool"),
        P("pool"),
    )
    out_specs = P(("pool", "tensor"), None)
    return jax.shard_map(shards, mesh=mesh, in_specs=in_specs, out_specs=out_specs, check_vma=False)
```

```python
import functools

import jax
import jax.numpy as jnp
from jax import lax
from jax.experimental import pallas as pl
from jax.experimental.pallas import tpu as pltpu
from jax.sharding import PartitionSpec as P

BLOCK = 128


adapter_scale_factor = 0.5


def tensor_shift(x, side, step, along_y):
    perm = []
    for yy in range(side):
        for xx in range(side):
            if along_y:
                perm.append((yy * side + xx, ((yy + step) % side) * side + xx))
            else:
                perm.append((yy * side + xx, yy * side + (xx + step) % side))
    return lax.ppermute(x, "tensor", perm)


def tensor_allsum(x, side):
    for along_y in (False, True):
        x = x + sum(tensor_shift(x, side, s, along_y) for s in range(1, side))
    return x


def scatter_kernel(count, rows, part_ref, recv_ref, send_sems, recv_sems):
    me = lax.axis_index("tensor")
    pool_me = lax.axis_index("pool")
    barrier = pltpu.get_barrier_semaphore()
    for d in range(1, count):
        other = lax.rem(me + d, count)
        pl.semaphore_signal(
            barrier, 1, device_id=(pool_me, other), device_id_type=pl.DeviceIdType.MESH
        )
    pl.semaphore_wait(barrier, count - 1)
    copies = []
    for d in range(1, count):
        target = lax.rem(me + d, count)
        start = pl.multiple_of(target * rows, rows)
        copy = pltpu.make_async_remote_copy(
            src_ref=part_ref.at[:, pl.ds(start, rows), :],
            dst_ref=recv_ref.at[d - 1],
            send_sem=send_sems.at[d - 1],
            recv_sem=recv_sems.at[d - 1],
            device_id=(pool_me, target),
            device_id_type=pl.DeviceIdType.MESH,
        )
        copy.start()
        copies.append(copy)
    for copy in copies:
        copy.wait()


def scatter_rows(partial_value, count, rows):
    chunks, _, width = partial_value.shape
    return pl.pallas_call(
        functools.partial(scatter_kernel, count, rows),
        out_shape=jax.ShapeDtypeStruct((count - 1, chunks, rows, width), partial_value.dtype),
        in_specs=[pl.BlockSpec(memory_space=pl.ANY)],
        out_specs=pl.BlockSpec(memory_space=pl.ANY),
        scratch_shapes=[
            pltpu.SemaphoreType.DMA((count - 1,)),
            pltpu.SemaphoreType.DMA((count - 1,)),
        ],
        compiler_params=pltpu.CompilerParams(collective_id=0, has_side_effects=True),
    )(partial_value)


def shards(hidden, down_weight, adapter_shrink, adapter_expand, block_adapter, block_rows):
    input_rows, feat = hidden.shape
    block_count = block_adapter.shape[0]
    pool_count = lax.axis_size("pool")
    tensor_pos = lax.axis_index("tensor")
    tensor_count = lax.axis_size("tensor")
    side = 4
    quarter = pool_count // side
    my_y = tensor_pos // side
    my_x = tensor_pos % side
    own_rows = input_rows // tensor_count
    held, _, rank = adapter_shrink.shape
    column_span = adapter_expand.shape[1]
    width = down_weight.shape[1]

    pairs = []
    for p1 in range(pool_count):
        for y1 in range(side):
            for x1 in range(side):
                y2 = p1 % side
                p2 = (p1 // side) * side + (y2 - y1) % side
                pairs.append((p1 * tensor_count + y1 * side + x1, p2 * tensor_count + y2 * side + x1))
    moved = lax.ppermute(down_weight, ("pool", "tensor"), pairs)

    shrink_rows = held * feat * rank // width
    expand_rows = held * column_span * rank // width
    pack = jnp.concatenate(
        [
            moved,
            adapter_shrink.reshape(shrink_rows, width),
            adapter_expand.reshape(expand_rows, width),
        ],
        axis=0,
    )
    gathered = lax.all_gather(pack, "pool", axis=0, tiled=False)
    plane_rows = gathered.shape[1]
    w_quarter = gathered.reshape(quarter, side, plane_rows, width)
    pieces = [hidden] + [tensor_shift(hidden, side, s, True) for s in range(1, side)]
    hidden_column = jnp.stack(pieces, axis=0).reshape(side, side, side, own_rows, feat)
    hidden_column = jnp.transpose(hidden_column, (2, 0, 1, 3, 4)).reshape(
        side, side, side * own_rows, feat
    )
    hidden_column = jnp.pad(hidden_column, ((0, 0), (0, 0), (0, 0), (0, plane_rows - feat)))

    shrink_part = shrink_rows // held
    expand_part = expand_rows // held
    first = jnp.stack([
        lax.dynamic_slice(
            gathered,
            (block_adapter[b] // held, feat + (block_adapter[b] % held) * shrink_part, 0),
            (1, shrink_part, width),
        )[0]
        for b in range(block_count)
    ]).reshape(block_count, feat, rank)
    second = jnp.stack([
        lax.dynamic_slice(
            gathered,
            (block_adapter[b] // held, feat + shrink_rows + (block_adapter[b] % held) * expand_part, 0),
            (1, expand_part, width),
        )[0]
        for b in range(block_count)
    ]).reshape(block_count, column_span, rank)
    blocks = hidden.reshape(block_count, BLOCK, feat)
    shrink = jnp.einsum("bnf,bfr->bnr", blocks, first, preferred_element_type=jnp.float32)
    summed_shrink = tensor_allsum(shrink, side).astype(jnp.bfloat16)
    enlarged_rows = jnp.einsum(
        "bnr,bcr->bnc", summed_shrink, second, preferred_element_type=jnp.float32
    )
    delta = (adapter_scale_factor * enlarged_rows).astype(jnp.bfloat16).reshape(input_rows, column_span)

    def rows_for(owner_x):
        rows = lax.dynamic_index_in_dim(hidden_column, owner_x, axis=0, keepdims=False)
        piece = jnp.einsum("sif,asfj->aij", rows, w_quarter, preferred_element_type=jnp.float32)
        return piece.astype(jnp.bfloat16).reshape(quarter, side, own_rows, width)

    total = None
    for s in range(1, side):
        arrived = tensor_shift(rows_for((my_x + s) % side), side, s, False).astype(jnp.float32)
        total = arrived if total is None else total + arrived
    total = (total + rows_for(my_x).astype(jnp.float32)).astype(jnp.bfloat16)

    got = [lax.dynamic_index_in_dim(total, my_y, axis=1, keepdims=False)]
    for s in range(1, side):
        piece = lax.dynamic_index_in_dim(total, (my_y + s) % side, axis=1, keepdims=False)
        got.append(tensor_shift(piece, side, s, True))
    order = (my_y - jnp.arange(side, dtype=jnp.int32)) % side
    result = jnp.take(jnp.stack(got, axis=0), order, axis=0)
    result = jnp.transpose(result, (2, 1, 0, 3)).reshape(own_rows, pool_count * width)
    delta_mine = lax.all_to_all(delta, "tensor", split_axis=0, concat_axis=1, tiled=True)
    result = (result.astype(jnp.float32) + delta_mine.astype(jnp.float32)).astype(jnp.bfloat16)

    row_ids = tensor_pos * own_rows + jnp.arange(own_rows, dtype=jnp.int32)
    owning = (row_ids // BLOCK)[:, None] == jnp.arange(block_count, dtype=jnp.int32)[None, :]
    lengths = jnp.sum(jnp.where(owning, block_rows[None, :], 0), axis=1)
    valid = row_ids % BLOCK < lengths
    return jnp.where(valid[:, None], result, jnp.zeros_like(result))


def solution(mesh):
    in_specs = (
        P("pool", "tensor"),
        P("tensor", "pool"),
        P("pool", "tensor", None),
        P("pool", "tensor", None),
        P("pool"),
        P("pool"),
    )
    out_specs = P(("pool", "tensor"), None)
    return jax.shard_map(shards, mesh=mesh, in_specs=in_specs, out_specs=out_specs, check_vma=False)
```

```python
import functools

import jax
import jax.numpy as jnp
from jax import lax
from jax.experimental import pallas as pl
from jax.experimental.pallas import tpu as pltpu
from jax.sharding import PartitionSpec as P

BLOCK = 128


adapter_scale_factor = 0.5


def tensor_shift(x, side, step, along_y):
    perm = []
    for yy in range(side):
        for xx in range(side):
            if along_y:
                perm.append((yy * side + xx, ((yy + step) % side) * side + xx))
            else:
                perm.append((yy * side + xx, yy * side + (xx + step) % side))
    return lax.ppermute(x, "tensor", perm)


def tensor_allsum(x, side):
    for along_y in (False, True):
        x = x + sum(tensor_shift(x, side, s, along_y) for s in range(1, side))
    return x


def scatter_kernel(count, rows, part_ref, recv_ref, send_sems, recv_sems):
    me = lax.axis_index("tensor")
    pool_me = lax.axis_index("pool")
    barrier = pltpu.get_barrier_semaphore()
    for d in range(1, count):
        other = lax.rem(me + d, count)
        pl.semaphore_signal(
            barrier, 1, device_id=(pool_me, other), device_id_type=pl.DeviceIdType.MESH
        )
    pl.semaphore_wait(barrier, count - 1)
    copies = []
    for d in range(1, count):
        target = lax.rem(me + d, count)
        start = pl.multiple_of(target * rows, rows)
        copy = pltpu.make_async_remote_copy(
            src_ref=part_ref.at[:, pl.ds(start, rows), :],
            dst_ref=recv_ref.at[d - 1],
            send_sem=send_sems.at[d - 1],
            recv_sem=recv_sems.at[d - 1],
            device_id=(pool_me, target),
            device_id_type=pl.DeviceIdType.MESH,
        )
        copy.start()
        copies.append(copy)
    for copy in copies:
        copy.wait()


def scatter_rows(partial_value, count, rows):
    chunks, _, width = partial_value.shape
    return pl.pallas_call(
        functools.partial(scatter_kernel, count, rows),
        out_shape=jax.ShapeDtypeStruct((count - 1, chunks, rows, width), partial_value.dtype),
        in_specs=[pl.BlockSpec(memory_space=pl.ANY)],
        out_specs=pl.BlockSpec(memory_space=pl.ANY),
        scratch_shapes=[
            pltpu.SemaphoreType.DMA((count - 1,)),
            pltpu.SemaphoreType.DMA((count - 1,)),
        ],
        compiler_params=pltpu.CompilerParams(collective_id=0, has_side_effects=True),
    )(partial_value)


def shards(hidden, down_weight, adapter_shrink, adapter_expand, block_adapter, block_rows):
    input_rows, feat = hidden.shape
    block_count = block_adapter.shape[0]
    pool_count = lax.axis_size("pool")
    tensor_pos = lax.axis_index("tensor")
    tensor_count = lax.axis_size("tensor")
    side = 4
    quarter = pool_count // side
    my_y = tensor_pos // side
    my_x = tensor_pos % side
    own_rows = input_rows // tensor_count
    held, _, rank = adapter_shrink.shape
    column_span = adapter_expand.shape[1]
    width = down_weight.shape[1]

    pairs = []
    for p1 in range(pool_count):
        for y1 in range(side):
            for x1 in range(side):
                y2 = p1 % side
                p2 = (p1 // side) * side + (y2 - y1) % side
                pairs.append((p1 * tensor_count + y1 * side + x1, p2 * tensor_count + y2 * side + x1))
    moved = lax.ppermute(down_weight, ("pool", "tensor"), pairs)

    half = width // 2
    shrink_rows = held * feat * rank // half
    expand_rows = held * column_span * rank // half
    pack = jnp.concatenate(
        [
            moved[:, :half],
            adapter_shrink.reshape(shrink_rows, half),
            adapter_expand.reshape(expand_rows, half),
        ],
        axis=0,
    )
    gathered = lax.all_gather(pack, "pool", axis=0, tiled=False)
    plane_rows = gathered.shape[1]
    w_first = gathered.reshape(quarter, side, plane_rows, half)
    shrink_all = gathered[:, feat:feat + shrink_rows, :].reshape(
        pool_count * held, shrink_rows // held, half
    )
    expand_all = gathered[:, feat + shrink_rows:, :].reshape(
        pool_count * held, expand_rows // held, half
    )
    w_second = lax.all_gather(moved[:, half:], "pool", axis=0, tiled=False).reshape(
        quarter, side, feat, half
    )

    pieces = [hidden] + [tensor_shift(hidden, side, s, True) for s in range(1, side)]
    hidden_column = jnp.stack(pieces, axis=0).reshape(side, side, side, own_rows, feat)
    hidden_column = jnp.transpose(hidden_column, (2, 0, 1, 3, 4)).reshape(
        side, side, side * own_rows, feat
    )
    hidden_padded = jnp.pad(hidden_column, ((0, 0), (0, 0), (0, 0), (0, plane_rows - feat)))

    first = jnp.take(shrink_all, block_adapter, axis=0).reshape(block_count, feat, rank)
    second = jnp.take(expand_all, block_adapter, axis=0).reshape(block_count, column_span, rank)
    blocks = hidden.reshape(block_count, BLOCK, feat)
    shrink = jnp.einsum("bnf,bfr->bnr", blocks, first, preferred_element_type=jnp.float32)
    summed_shrink = tensor_allsum(shrink, side).astype(jnp.bfloat16)
    enlarged_rows = jnp.einsum(
        "bnr,bcr->bnc", summed_shrink, second, preferred_element_type=jnp.float32
    )
    delta = (adapter_scale_factor * enlarged_rows).astype(jnp.bfloat16).reshape(input_rows, column_span)

    def reduce_over_x(hidden_rows, w_half):
        def rows_for(owner_x):
            rows = lax.dynamic_index_in_dim(hidden_rows, owner_x, axis=0, keepdims=False)
            piece = jnp.einsum("sif,asfj->aij", rows, w_half, preferred_element_type=jnp.float32)
            return piece.astype(jnp.bfloat16).reshape(quarter, side, own_rows, half)

        summed = None
        for s in range(1, side):
            arrived = tensor_shift(rows_for((my_x + s) % side), side, s, False).astype(jnp.float32)
            summed = arrived if summed is None else summed + arrived
        return (summed + rows_for(my_x).astype(jnp.float32)).astype(jnp.bfloat16)

    total = jnp.concatenate(
        [reduce_over_x(hidden_padded, w_first), reduce_over_x(hidden_column, w_second)], axis=3
    )

    got = [lax.dynamic_index_in_dim(total, my_y, axis=1, keepdims=False)]
    for s in range(1, side):
        piece = lax.dynamic_index_in_dim(total, (my_y + s) % side, axis=1, keepdims=False)
        got.append(tensor_shift(piece, side, s, True))
    order = (my_y - jnp.arange(side, dtype=jnp.int32)) % side
    result = jnp.take(jnp.stack(got, axis=0), order, axis=0)
    result = jnp.transpose(result, (2, 1, 0, 3)).reshape(own_rows, pool_count * width)
    delta_mine = lax.all_to_all(delta, "tensor", split_axis=0, concat_axis=1, tiled=True)
    result = (result.astype(jnp.float32) + delta_mine.astype(jnp.float32)).astype(jnp.bfloat16)

    row_ids = tensor_pos * own_rows + jnp.arange(own_rows, dtype=jnp.int32)
    owning = (row_ids // BLOCK)[:, None] == jnp.arange(block_count, dtype=jnp.int32)[None, :]
    lengths = jnp.sum(jnp.where(owning, block_rows[None, :], 0), axis=1)
    valid = row_ids % BLOCK < lengths
    return jnp.where(valid[:, None], result, jnp.zeros_like(result))


def solution(mesh):
    in_specs = (
        P("pool", "tensor"),
        P("tensor", "pool"),
        P("pool", "tensor", None),
        P("pool", "tensor", None),
        P("pool"),
        P("pool"),
    )
    out_specs = P(("pool", "tensor"), None)
    return jax.shard_map(shards, mesh=mesh, in_specs=in_specs, out_specs=out_specs, check_vma=False)
```

```python
import functools

import jax
import jax.numpy as jnp
from jax import lax
from jax.experimental import pallas as pl
from jax.experimental.pallas import tpu as pltpu
from jax.sharding import PartitionSpec as P

BLOCK = 128


adapter_scale_factor = 0.5


def tensor_shift(x, side, step, along_y):
    perm = []
    for yy in range(side):
        for xx in range(side):
            if along_y:
                perm.append((yy * side + xx, ((yy + step) % side) * side + xx))
            else:
                perm.append((yy * side + xx, yy * side + (xx + step) % side))
    return lax.ppermute(x, "tensor", perm)


def tensor_allsum(x, side):
    for along_y in (False, True):
        x = x + sum(tensor_shift(x, side, s, along_y) for s in range(1, side))
    return x


def scatter_kernel(count, rows, part_ref, recv_ref, send_sems, recv_sems):
    me = lax.axis_index("tensor")
    pool_me = lax.axis_index("pool")
    barrier = pltpu.get_barrier_semaphore()
    for d in range(1, count):
        other = lax.rem(me + d, count)
        pl.semaphore_signal(
            barrier, 1, device_id=(pool_me, other), device_id_type=pl.DeviceIdType.MESH
        )
    pl.semaphore_wait(barrier, count - 1)
    copies = []
    for d in range(1, count):
        target = lax.rem(me + d, count)
        start = pl.multiple_of(target * rows, rows)
        copy = pltpu.make_async_remote_copy(
            src_ref=part_ref.at[:, pl.ds(start, rows), :],
            dst_ref=recv_ref.at[d - 1],
            send_sem=send_sems.at[d - 1],
            recv_sem=recv_sems.at[d - 1],
            device_id=(pool_me, target),
            device_id_type=pl.DeviceIdType.MESH,
        )
        copy.start()
        copies.append(copy)
    for copy in copies:
        copy.wait()


def scatter_rows(partial_value, count, rows):
    chunks, _, width = partial_value.shape
    return pl.pallas_call(
        functools.partial(scatter_kernel, count, rows),
        out_shape=jax.ShapeDtypeStruct((count - 1, chunks, rows, width), partial_value.dtype),
        in_specs=[pl.BlockSpec(memory_space=pl.ANY)],
        out_specs=pl.BlockSpec(memory_space=pl.ANY),
        scratch_shapes=[
            pltpu.SemaphoreType.DMA((count - 1,)),
            pltpu.SemaphoreType.DMA((count - 1,)),
        ],
        compiler_params=pltpu.CompilerParams(collective_id=0, has_side_effects=True),
    )(partial_value)


def shards(hidden, down_weight, adapter_shrink, adapter_expand, block_adapter, block_rows):
    input_rows, feat = hidden.shape
    block_count = block_adapter.shape[0]
    pool_count = lax.axis_size("pool")
    tensor_pos = lax.axis_index("tensor")
    tensor_count = lax.axis_size("tensor")
    side = 4
    quarter = pool_count // side
    my_y = tensor_pos // side
    my_x = tensor_pos % side
    own_rows = input_rows // tensor_count
    held, _, rank = adapter_shrink.shape
    column_span = adapter_expand.shape[1]
    width = down_weight.shape[1]

    pairs = []
    for p1 in range(pool_count):
        for y1 in range(side):
            for x1 in range(side):
                y2 = p1 % side
                p2 = (p1 // side) * side + (y2 - y1) % side
                pairs.append((p1 * tensor_count + y1 * side + x1, p2 * tensor_count + y2 * side + x1))
    moved = lax.ppermute(down_weight, ("pool", "tensor"), pairs)

    half = width // 2
    shrink_rows = held * feat * rank // half
    expand_rows = held * column_span * rank // half
    pack = jnp.concatenate(
        [
            moved[:, :half],
            adapter_shrink.reshape(shrink_rows, half),
            adapter_expand.reshape(expand_rows, half),
        ],
        axis=0,
    )
    gathered = lax.all_gather(pack, "pool", axis=0, tiled=False)
    later, gathered = lax.optimization_barrier((moved[:, half:], gathered))
    plane_rows = gathered.shape[1]
    w_first = gathered.reshape(quarter, side, plane_rows, half)
    shrink_all = gathered[:, feat:feat + shrink_rows, :].reshape(
        pool_count * held, shrink_rows // held, half
    )
    expand_all = gathered[:, feat + shrink_rows:, :].reshape(
        pool_count * held, expand_rows // held, half
    )
    w_second = lax.all_gather(later, "pool", axis=0, tiled=False).reshape(
        quarter, side, feat, half
    )

    pieces = [hidden] + [tensor_shift(hidden, side, s, True) for s in range(1, side)]
    hidden_column = jnp.stack(pieces, axis=0).reshape(side, side, side, own_rows, feat)
    hidden_column = jnp.transpose(hidden_column, (2, 0, 1, 3, 4)).reshape(
        side, side, side * own_rows, feat
    )
    hidden_padded = jnp.pad(hidden_column, ((0, 0), (0, 0), (0, 0), (0, plane_rows - feat)))

    first = jnp.take(shrink_all, block_adapter, axis=0).reshape(block_count, feat, rank)
    second = jnp.take(expand_all, block_adapter, axis=0).reshape(block_count, column_span, rank)
    blocks = hidden.reshape(block_count, BLOCK, feat)
    shrink = jnp.einsum("bnf,bfr->bnr", blocks, first, preferred_element_type=jnp.float32)
    summed_shrink = tensor_allsum(shrink, side).astype(jnp.bfloat16)
    enlarged_rows = jnp.einsum(
        "bnr,bcr->bnc", summed_shrink, second, preferred_element_type=jnp.float32
    )
    delta = (adapter_scale_factor * enlarged_rows).astype(jnp.bfloat16).reshape(input_rows, column_span)

    def reduce_over_x(hidden_rows, w_half):
        def rows_for(owner_x):
            rows = lax.dynamic_index_in_dim(hidden_rows, owner_x, axis=0, keepdims=False)
            piece = jnp.einsum("sif,asfj->aij", rows, w_half, preferred_element_type=jnp.float32)
            return piece.astype(jnp.bfloat16).reshape(quarter, side, own_rows, half)

        summed = None
        for s in range(1, side):
            arrived = tensor_shift(rows_for((my_x + s) % side), side, s, False).astype(jnp.float32)
            summed = arrived if summed is None else summed + arrived
        return (summed + rows_for(my_x).astype(jnp.float32)).astype(jnp.bfloat16)

    total = jnp.concatenate(
        [reduce_over_x(hidden_padded, w_first), reduce_over_x(hidden_column, w_second)], axis=3
    )

    got = [lax.dynamic_index_in_dim(total, my_y, axis=1, keepdims=False)]
    for s in range(1, side):
        piece = lax.dynamic_index_in_dim(total, (my_y + s) % side, axis=1, keepdims=False)
        got.append(tensor_shift(piece, side, s, True))
    order = (my_y - jnp.arange(side, dtype=jnp.int32)) % side
    result = jnp.take(jnp.stack(got, axis=0), order, axis=0)
    result = jnp.transpose(result, (2, 1, 0, 3)).reshape(own_rows, pool_count * width)
    delta_mine = lax.all_to_all(delta, "tensor", split_axis=0, concat_axis=1, tiled=True)
    result = (result.astype(jnp.float32) + delta_mine.astype(jnp.float32)).astype(jnp.bfloat16)

    row_ids = tensor_pos * own_rows + jnp.arange(own_rows, dtype=jnp.int32)
    owning = (row_ids // BLOCK)[:, None] == jnp.arange(block_count, dtype=jnp.int32)[None, :]
    lengths = jnp.sum(jnp.where(owning, block_rows[None, :], 0), axis=1)
    valid = row_ids % BLOCK < lengths
    return jnp.where(valid[:, None], result, jnp.zeros_like(result))


def solution(mesh):
    in_specs = (
        P("pool", "tensor"),
        P("tensor", "pool"),
        P("pool", "tensor", None),
        P("pool", "tensor", None),
        P("pool"),
        P("pool"),
    )
    out_specs = P(("pool", "tensor"), None)
    return jax.shard_map(shards, mesh=mesh, in_specs=in_specs, out_specs=out_specs, check_vma=False)
```

```python
import functools

import jax
import jax.numpy as jnp
from jax import lax
from jax.experimental import pallas as pl
from jax.experimental.pallas import tpu as pltpu
from jax.sharding import PartitionSpec as P

BLOCK = 128


adapter_scale_factor = 0.5


def tensor_shift(x, side, step, along_y):
    perm = []
    for yy in range(side):
        for xx in range(side):
            if along_y:
                perm.append((yy * side + xx, ((yy + step) % side) * side + xx))
            else:
                perm.append((yy * side + xx, yy * side + (xx + step) % side))
    return lax.ppermute(x, "tensor", perm)


def tensor_allsum(x, side):
    for along_y in (False, True):
        x = x + sum(tensor_shift(x, side, s, along_y) for s in range(1, side))
    return x


def scatter_kernel(count, rows, part_ref, recv_ref, send_sems, recv_sems):
    me = lax.axis_index("tensor")
    pool_me = lax.axis_index("pool")
    barrier = pltpu.get_barrier_semaphore()
    for d in range(1, count):
        other = lax.rem(me + d, count)
        pl.semaphore_signal(
            barrier, 1, device_id=(pool_me, other), device_id_type=pl.DeviceIdType.MESH
        )
    pl.semaphore_wait(barrier, count - 1)
    copies = []
    for d in range(1, count):
        target = lax.rem(me + d, count)
        start = pl.multiple_of(target * rows, rows)
        copy = pltpu.make_async_remote_copy(
            src_ref=part_ref.at[:, pl.ds(start, rows), :],
            dst_ref=recv_ref.at[d - 1],
            send_sem=send_sems.at[d - 1],
            recv_sem=recv_sems.at[d - 1],
            device_id=(pool_me, target),
            device_id_type=pl.DeviceIdType.MESH,
        )
        copy.start()
        copies.append(copy)
    for copy in copies:
        copy.wait()


def scatter_rows(partial_value, count, rows):
    chunks, _, width = partial_value.shape
    return pl.pallas_call(
        functools.partial(scatter_kernel, count, rows),
        out_shape=jax.ShapeDtypeStruct((count - 1, chunks, rows, width), partial_value.dtype),
        in_specs=[pl.BlockSpec(memory_space=pl.ANY)],
        out_specs=pl.BlockSpec(memory_space=pl.ANY),
        scratch_shapes=[
            pltpu.SemaphoreType.DMA((count - 1,)),
            pltpu.SemaphoreType.DMA((count - 1,)),
        ],
        compiler_params=pltpu.CompilerParams(collective_id=0, has_side_effects=True),
    )(partial_value)


def shards(hidden, down_weight, adapter_shrink, adapter_expand, block_adapter, block_rows):
    input_rows, feat = hidden.shape
    block_count = block_adapter.shape[0]
    pool_count = lax.axis_size("pool")
    tensor_pos = lax.axis_index("tensor")
    tensor_count = lax.axis_size("tensor")
    side = 4
    quarter = pool_count // side
    my_y = tensor_pos // side
    my_x = tensor_pos % side
    own_rows = input_rows // tensor_count
    held, _, rank = adapter_shrink.shape
    column_span = adapter_expand.shape[1]
    width = down_weight.shape[1]

    pairs = []
    for p1 in range(pool_count):
        for y1 in range(side):
            for x1 in range(side):
                y2 = p1 % side
                p2 = (p1 // side) * side + (y2 - y1) % side
                pairs.append((p1 * tensor_count + y1 * side + x1, p2 * tensor_count + y2 * side + x1))
    moved = lax.ppermute(down_weight, ("pool", "tensor"), pairs)

    half = width // 2
    shrink_rows = held * feat * rank // half
    expand_rows = held * column_span * rank // half
    pack = jnp.concatenate(
        [
            moved[:, :half],
            adapter_shrink.reshape(shrink_rows, half),
            adapter_expand.reshape(expand_rows, half),
        ],
        axis=0,
    )
    gathered = lax.all_gather(pack, "pool", axis=0, tiled=False)
    pieces = [hidden] + [tensor_shift(hidden, side, s, True) for s in range(1, side)]
    later, gathered, pieces = lax.optimization_barrier((moved[:, half:], gathered, pieces))
    plane_rows = gathered.shape[1]
    w_first = gathered.reshape(quarter, side, plane_rows, half)
    shrink_all = gathered[:, feat:feat + shrink_rows, :].reshape(
        pool_count * held, shrink_rows // held, half
    )
    expand_all = gathered[:, feat + shrink_rows:, :].reshape(
        pool_count * held, expand_rows // held, half
    )
    w_second = lax.all_gather(later, "pool", axis=0, tiled=False).reshape(
        quarter, side, feat, half
    )

    hidden_column = jnp.stack(pieces, axis=0).reshape(side, side, side, own_rows, feat)
    hidden_column = jnp.transpose(hidden_column, (2, 0, 1, 3, 4)).reshape(
        side, side, side * own_rows, feat
    )
    hidden_padded = jnp.pad(hidden_column, ((0, 0), (0, 0), (0, 0), (0, plane_rows - feat)))

    first = jnp.take(shrink_all, block_adapter, axis=0).reshape(block_count, feat, rank)
    second = jnp.take(expand_all, block_adapter, axis=0).reshape(block_count, column_span, rank)
    blocks = hidden.reshape(block_count, BLOCK, feat)
    shrink = jnp.einsum("bnf,bfr->bnr", blocks, first, preferred_element_type=jnp.float32)
    summed_shrink = tensor_allsum(shrink, side).astype(jnp.bfloat16)
    enlarged_rows = jnp.einsum(
        "bnr,bcr->bnc", summed_shrink, second, preferred_element_type=jnp.float32
    )
    delta = (adapter_scale_factor * enlarged_rows).astype(jnp.bfloat16).reshape(input_rows, column_span)

    def reduce_over_x(hidden_rows, w_half):
        def rows_for(owner_x):
            rows = lax.dynamic_index_in_dim(hidden_rows, owner_x, axis=0, keepdims=False)
            piece = jnp.einsum("sif,asfj->aij", rows, w_half, preferred_element_type=jnp.float32)
            return piece.astype(jnp.bfloat16).reshape(quarter, side, own_rows, half)

        summed = None
        for s in range(1, side):
            arrived = tensor_shift(rows_for((my_x + s) % side), side, s, False).astype(jnp.float32)
            summed = arrived if summed is None else summed + arrived
        return (summed + rows_for(my_x).astype(jnp.float32)).astype(jnp.bfloat16)

    total = jnp.concatenate(
        [reduce_over_x(hidden_padded, w_first), reduce_over_x(hidden_column, w_second)], axis=3
    )

    got = [lax.dynamic_index_in_dim(total, my_y, axis=1, keepdims=False)]
    for s in range(1, side):
        piece = lax.dynamic_index_in_dim(total, (my_y + s) % side, axis=1, keepdims=False)
        got.append(tensor_shift(piece, side, s, True))
    order = (my_y - jnp.arange(side, dtype=jnp.int32)) % side
    result = jnp.take(jnp.stack(got, axis=0), order, axis=0)
    result = jnp.transpose(result, (2, 1, 0, 3)).reshape(own_rows, pool_count * width)
    delta_mine = lax.all_to_all(delta, "tensor", split_axis=0, concat_axis=1, tiled=True)
    result = (result.astype(jnp.float32) + delta_mine.astype(jnp.float32)).astype(jnp.bfloat16)

    row_ids = tensor_pos * own_rows + jnp.arange(own_rows, dtype=jnp.int32)
    owning = (row_ids // BLOCK)[:, None] == jnp.arange(block_count, dtype=jnp.int32)[None, :]
    lengths = jnp.sum(jnp.where(owning, block_rows[None, :], 0), axis=1)
    valid = row_ids % BLOCK < lengths
    return jnp.where(valid[:, None], result, jnp.zeros_like(result))


def solution(mesh):
    in_specs = (
        P("pool", "tensor"),
        P("tensor", "pool"),
        P("pool", "tensor", None),
        P("pool", "tensor", None),
        P("pool"),
        P("pool"),
    )
    out_specs = P(("pool", "tensor"), None)
    return jax.shard_map(shards, mesh=mesh, in_specs=in_specs, out_specs=out_specs, check_vma=False)
```

```python
import functools

import jax
import jax.numpy as jnp
from jax import lax
from jax.experimental import pallas as pl
from jax.experimental.pallas import tpu as pltpu
from jax.sharding import PartitionSpec as P

BLOCK = 128


adapter_scale_factor = 0.5


def tensor_shift(x, side, step, along_y):
    perm = []
    for yy in range(side):
        for xx in range(side):
            if along_y:
                perm.append((yy * side + xx, ((yy + step) % side) * side + xx))
            else:
                perm.append((yy * side + xx, yy * side + (xx + step) % side))
    return lax.ppermute(x, "tensor", perm)


def tensor_allsum(x, side):
    for along_y in (False, True):
        x = x + sum(tensor_shift(x, side, s, along_y) for s in range(1, side))
    return x


def scatter_kernel(count, rows, part_ref, recv_ref, send_sems, recv_sems):
    me = lax.axis_index("tensor")
    pool_me = lax.axis_index("pool")
    barrier = pltpu.get_barrier_semaphore()
    for d in range(1, count):
        other = lax.rem(me + d, count)
        pl.semaphore_signal(
            barrier, 1, device_id=(pool_me, other), device_id_type=pl.DeviceIdType.MESH
        )
    pl.semaphore_wait(barrier, count - 1)
    copies = []
    for d in range(1, count):
        target = lax.rem(me + d, count)
        start = pl.multiple_of(target * rows, rows)
        copy = pltpu.make_async_remote_copy(
            src_ref=part_ref.at[:, pl.ds(start, rows), :],
            dst_ref=recv_ref.at[d - 1],
            send_sem=send_sems.at[d - 1],
            recv_sem=recv_sems.at[d - 1],
            device_id=(pool_me, target),
            device_id_type=pl.DeviceIdType.MESH,
        )
        copy.start()
        copies.append(copy)
    for copy in copies:
        copy.wait()


def scatter_rows(partial_value, count, rows):
    chunks, _, width = partial_value.shape
    return pl.pallas_call(
        functools.partial(scatter_kernel, count, rows),
        out_shape=jax.ShapeDtypeStruct((count - 1, chunks, rows, width), partial_value.dtype),
        in_specs=[pl.BlockSpec(memory_space=pl.ANY)],
        out_specs=pl.BlockSpec(memory_space=pl.ANY),
        scratch_shapes=[
            pltpu.SemaphoreType.DMA((count - 1,)),
            pltpu.SemaphoreType.DMA((count - 1,)),
        ],
        compiler_params=pltpu.CompilerParams(collective_id=0, has_side_effects=True),
    )(partial_value)


def shards(hidden, down_weight, adapter_shrink, adapter_expand, block_adapter, block_rows):
    input_rows, feat = hidden.shape
    block_count = block_adapter.shape[0]
    pool_count = lax.axis_size("pool")
    tensor_pos = lax.axis_index("tensor")
    tensor_count = lax.axis_size("tensor")
    side = 4
    quarter = pool_count // side
    my_y = tensor_pos // side
    my_x = tensor_pos % side
    own_rows = input_rows // tensor_count
    held, _, rank = adapter_shrink.shape
    column_span = adapter_expand.shape[1]
    width = down_weight.shape[1]

    pairs = []
    for p1 in range(pool_count):
        for y1 in range(side):
            for x1 in range(side):
                y2 = p1 % side
                p2 = (p1 // side) * side + (y2 - y1) % side
                pairs.append((p1 * tensor_count + y1 * side + x1, p2 * tensor_count + y2 * side + x1))
    moved = lax.ppermute(down_weight, ("pool", "tensor"), pairs)

    half = width // 2
    shrink_rows = held * feat * rank // half
    expand_rows = held * column_span * rank // half
    pack = jnp.concatenate(
        [
            moved[:, :half],
            adapter_shrink.reshape(shrink_rows, half),
            adapter_expand.reshape(expand_rows, half),
        ],
        axis=0,
    )
    gathered = lax.all_gather(pack, "pool", axis=0, tiled=False)
    pieces = [hidden] + [tensor_shift(hidden, side, s, True) for s in range(1, side)]
    later, gathered, pieces = lax.optimization_barrier((moved[:, half:], gathered, pieces))
    plane_rows = gathered.shape[1]
    w_first = gathered.reshape(quarter, side, plane_rows, half)
    shrink_all = gathered[:, feat:feat + shrink_rows, :].reshape(
        pool_count * held, shrink_rows // held, half
    )
    expand_all = gathered[:, feat + shrink_rows:, :].reshape(
        pool_count * held, expand_rows // held, half
    )
    w_second = lax.all_gather(later, "pool", axis=0, tiled=False).reshape(
        quarter, side, feat, half
    )

    hidden_column = jnp.stack(pieces, axis=0).reshape(side, side, side, own_rows, feat)
    hidden_column = jnp.transpose(hidden_column, (2, 0, 1, 3, 4)).reshape(
        side, side, side * own_rows, feat
    )
    hidden_padded = jnp.pad(hidden_column, ((0, 0), (0, 0), (0, 0), (0, plane_rows - feat)))

    first = jnp.take(shrink_all, block_adapter, axis=0).reshape(block_count, feat, rank)
    second = jnp.take(expand_all, block_adapter, axis=0).reshape(block_count, column_span, rank)
    blocks = hidden.reshape(block_count, BLOCK, feat)
    shrink = jnp.einsum("bnf,bfr->bnr", blocks, first, preferred_element_type=jnp.float32)
    summed_shrink = tensor_allsum(shrink, side).astype(jnp.bfloat16)
    enlarged_rows = jnp.einsum(
        "bnr,bcr->bnc", summed_shrink, second, preferred_element_type=jnp.float32
    )
    delta = (adapter_scale_factor * enlarged_rows).astype(jnp.bfloat16).reshape(input_rows, column_span)

    def reduce_over_x(hidden_rows, w_half):
        def rows_for(owner_x):
            rows = lax.dynamic_index_in_dim(hidden_rows, owner_x, axis=0, keepdims=False)
            piece = jnp.einsum("sif,asfj->aij", rows, w_half, preferred_element_type=jnp.float32)
            return piece.astype(jnp.bfloat16).reshape(quarter, side, own_rows, half)

        summed = None
        for s in range(1, side):
            arrived = tensor_shift(rows_for((my_x + s) % side), side, s, False).astype(jnp.float32)
            summed = arrived if summed is None else summed + arrived
        return (summed + rows_for(my_x).astype(jnp.float32)).astype(jnp.bfloat16)

    order = (my_y - jnp.arange(side, dtype=jnp.int32)) % side

    def exchange_over_y(total):
        got = [lax.dynamic_index_in_dim(total, my_y, axis=1, keepdims=False)]
        for s in range(1, side):
            piece = lax.dynamic_index_in_dim(total, (my_y + s) % side, axis=1, keepdims=False)
            got.append(tensor_shift(piece, side, s, True))
        return jnp.transpose(jnp.take(jnp.stack(got, axis=0), order, axis=0), (2, 1, 0, 3))

    result = jnp.concatenate(
        [
            exchange_over_y(reduce_over_x(hidden_padded, w_first)),
            exchange_over_y(reduce_over_x(hidden_column, w_second)),
        ],
        axis=3,
    ).reshape(own_rows, pool_count * width)
    delta_mine = lax.all_to_all(delta, "tensor", split_axis=0, concat_axis=1, tiled=True)
    result = (result.astype(jnp.float32) + delta_mine.astype(jnp.float32)).astype(jnp.bfloat16)

    row_ids = tensor_pos * own_rows + jnp.arange(own_rows, dtype=jnp.int32)
    owning = (row_ids // BLOCK)[:, None] == jnp.arange(block_count, dtype=jnp.int32)[None, :]
    lengths = jnp.sum(jnp.where(owning, block_rows[None, :], 0), axis=1)
    valid = row_ids % BLOCK < lengths
    return jnp.where(valid[:, None], result, jnp.zeros_like(result))


def solution(mesh):
    in_specs = (
        P("pool", "tensor"),
        P("tensor", "pool"),
        P("pool", "tensor", None),
        P("pool", "tensor", None),
        P("pool"),
        P("pool"),
    )
    out_specs = P(("pool", "tensor"), None)
    return jax.shard_map(shards, mesh=mesh, in_specs=in_specs, out_specs=out_specs, check_vma=False)
```

```python
import functools

import jax
import jax.numpy as jnp
from jax import lax
from jax.experimental import pallas as pl
from jax.experimental.pallas import tpu as pltpu
from jax.sharding import PartitionSpec as P

BLOCK = 128


adapter_scale_factor = 0.5


def tensor_shift(x, side, step, along_y):
    perm = []
    for yy in range(side):
        for xx in range(side):
            if along_y:
                perm.append((yy * side + xx, ((yy + step) % side) * side + xx))
            else:
                perm.append((yy * side + xx, yy * side + (xx + step) % side))
    return lax.ppermute(x, "tensor", perm)


def tensor_allsum(x, side):
    for along_y in (False, True):
        x = x + sum(tensor_shift(x, side, s, along_y) for s in range(1, side))
    return x


def scatter_kernel(count, rows, part_ref, recv_ref, send_sems, recv_sems):
    me = lax.axis_index("tensor")
    pool_me = lax.axis_index("pool")
    barrier = pltpu.get_barrier_semaphore()
    for d in range(1, count):
        other = lax.rem(me + d, count)
        pl.semaphore_signal(
            barrier, 1, device_id=(pool_me, other), device_id_type=pl.DeviceIdType.MESH
        )
    pl.semaphore_wait(barrier, count - 1)
    copies = []
    for d in range(1, count):
        target = lax.rem(me + d, count)
        start = pl.multiple_of(target * rows, rows)
        copy = pltpu.make_async_remote_copy(
            src_ref=part_ref.at[:, pl.ds(start, rows), :],
            dst_ref=recv_ref.at[d - 1],
            send_sem=send_sems.at[d - 1],
            recv_sem=recv_sems.at[d - 1],
            device_id=(pool_me, target),
            device_id_type=pl.DeviceIdType.MESH,
        )
        copy.start()
        copies.append(copy)
    for copy in copies:
        copy.wait()


def scatter_rows(partial_value, count, rows):
    chunks, _, width = partial_value.shape
    return pl.pallas_call(
        functools.partial(scatter_kernel, count, rows),
        out_shape=jax.ShapeDtypeStruct((count - 1, chunks, rows, width), partial_value.dtype),
        in_specs=[pl.BlockSpec(memory_space=pl.ANY)],
        out_specs=pl.BlockSpec(memory_space=pl.ANY),
        scratch_shapes=[
            pltpu.SemaphoreType.DMA((count - 1,)),
            pltpu.SemaphoreType.DMA((count - 1,)),
        ],
        compiler_params=pltpu.CompilerParams(collective_id=0, has_side_effects=True),
    )(partial_value)


def shards(hidden, down_weight, adapter_shrink, adapter_expand, block_adapter, block_rows):
    input_rows, feat = hidden.shape
    block_count = block_adapter.shape[0]
    pool_count = lax.axis_size("pool")
    tensor_pos = lax.axis_index("tensor")
    tensor_count = lax.axis_size("tensor")
    side = 4
    quarter = pool_count // side
    my_y = tensor_pos // side
    my_x = tensor_pos % side
    own_rows = input_rows // tensor_count
    held, _, rank = adapter_shrink.shape
    column_span = adapter_expand.shape[1]
    width = down_weight.shape[1]

    pairs = []
    for p1 in range(pool_count):
        for y1 in range(side):
            for x1 in range(side):
                y2 = p1 % side
                p2 = (p1 // side) * side + (y2 - y1) % side
                pairs.append((p1 * tensor_count + y1 * side + x1, p2 * tensor_count + y2 * side + x1))
    moved = lax.ppermute(down_weight, ("pool", "tensor"), pairs)

    half = width // 2
    shrink_rows = held * feat * rank // half
    expand_rows = held * column_span * rank // half
    pack = jnp.concatenate(
        [
            moved[:, :half],
            adapter_shrink.reshape(shrink_rows, half),
            adapter_expand.reshape(expand_rows, half),
        ],
        axis=0,
    )
    gathered = lax.all_gather(pack, "pool", axis=0, tiled=False)
    pieces = [hidden] + [tensor_shift(hidden, side, s, True) for s in range(1, side)]
    later, gathered, pieces = lax.optimization_barrier((moved[:, half:], gathered, pieces))
    plane_rows = gathered.shape[1]
    w_first = gathered.reshape(quarter, side, plane_rows, half)
    w_second = lax.all_gather(later, "pool", axis=0, tiled=False).reshape(
        quarter, side, feat, half
    )

    hidden_column = jnp.stack(pieces, axis=0).reshape(side, side, side, own_rows, feat)
    hidden_column = jnp.transpose(hidden_column, (2, 0, 1, 3, 4)).reshape(
        side, side, side * own_rows, feat
    )
    hidden_padded = jnp.pad(hidden_column, ((0, 0), (0, 0), (0, 0), (0, plane_rows - feat)))

    shrink_part = shrink_rows // held
    expand_part = expand_rows // held
    first = jnp.stack([
        lax.dynamic_slice(
            gathered,
            (block_adapter[b] // held, feat + (block_adapter[b] % held) * shrink_part, 0),
            (1, shrink_part, half),
        )[0]
        for b in range(block_count)
    ]).reshape(block_count, feat, rank)
    second = jnp.stack([
        lax.dynamic_slice(
            gathered,
            (block_adapter[b] // held, feat + shrink_rows + (block_adapter[b] % held) * expand_part, 0),
            (1, expand_part, half),
        )[0]
        for b in range(block_count)
    ]).reshape(block_count, column_span, rank)
    blocks = hidden.reshape(block_count, BLOCK, feat)
    shrink = jnp.einsum("bnf,bfr->bnr", blocks, first, preferred_element_type=jnp.float32)
    summed_shrink = tensor_allsum(shrink, side).astype(jnp.bfloat16)
    enlarged_rows = jnp.einsum(
        "bnr,bcr->bnc", summed_shrink, second, preferred_element_type=jnp.float32
    )
    delta = (adapter_scale_factor * enlarged_rows).astype(jnp.bfloat16).reshape(input_rows, column_span)

    def reduce_over_x(hidden_rows, w_half):
        def rows_for(owner_x):
            rows = lax.dynamic_index_in_dim(hidden_rows, owner_x, axis=0, keepdims=False)
            piece = jnp.einsum("sif,asfj->aij", rows, w_half, preferred_element_type=jnp.float32)
            return piece.astype(jnp.bfloat16).reshape(quarter, side, own_rows, half)

        summed = None
        for s in range(1, side):
            arrived = tensor_shift(rows_for((my_x + s) % side), side, s, False).astype(jnp.float32)
            summed = arrived if summed is None else summed + arrived
        return (summed + rows_for(my_x).astype(jnp.float32)).astype(jnp.bfloat16)

    order = (my_y - jnp.arange(side, dtype=jnp.int32)) % side

    def exchange_over_y(total):
        got = [lax.dynamic_index_in_dim(total, my_y, axis=1, keepdims=False)]
        for s in range(1, side):
            piece = lax.dynamic_index_in_dim(total, (my_y + s) % side, axis=1, keepdims=False)
            got.append(tensor_shift(piece, side, s, True))
        return jnp.transpose(jnp.take(jnp.stack(got, axis=0), order, axis=0), (2, 1, 0, 3))

    result = jnp.concatenate(
        [
            exchange_over_y(reduce_over_x(hidden_padded, w_first)),
            exchange_over_y(reduce_over_x(hidden_column, w_second)),
        ],
        axis=3,
    ).reshape(own_rows, pool_count * width)
    delta_mine = lax.all_to_all(delta, "tensor", split_axis=0, concat_axis=1, tiled=True)
    result = (result.astype(jnp.float32) + delta_mine.astype(jnp.float32)).astype(jnp.bfloat16)

    row_ids = tensor_pos * own_rows + jnp.arange(own_rows, dtype=jnp.int32)
    owning = (row_ids // BLOCK)[:, None] == jnp.arange(block_count, dtype=jnp.int32)[None, :]
    lengths = jnp.sum(jnp.where(owning, block_rows[None, :], 0), axis=1)
    valid = row_ids % BLOCK < lengths
    return jnp.where(valid[:, None], result, jnp.zeros_like(result))


def solution(mesh):
    in_specs = (
        P("pool", "tensor"),
        P("tensor", "pool"),
        P("pool", "tensor", None),
        P("pool", "tensor", None),
        P("pool"),
        P("pool"),
    )
    out_specs = P(("pool", "tensor"), None)
    return jax.shard_map(shards, mesh=mesh, in_specs=in_specs, out_specs=out_specs, check_vma=False)
```

```python
import functools

import jax
import jax.numpy as jnp
from jax import lax
from jax.experimental import pallas as pl
from jax.experimental.pallas import tpu as pltpu
from jax.sharding import PartitionSpec as P

BLOCK = 128


adapter_scale_factor = 0.5


def tensor_shift(x, side, step, along_y):
    perm = []
    for yy in range(side):
        for xx in range(side):
            if along_y:
                perm.append((yy * side + xx, ((yy + step) % side) * side + xx))
            else:
                perm.append((yy * side + xx, yy * side + (xx + step) % side))
    return lax.ppermute(x, "tensor", perm)


def tensor_allsum(x, side):
    for along_y in (False, True):
        x = x + sum(tensor_shift(x, side, s, along_y) for s in range(1, side))
    return x


def scatter_kernel(count, rows, part_ref, recv_ref, send_sems, recv_sems):
    me = lax.axis_index("tensor")
    pool_me = lax.axis_index("pool")
    barrier = pltpu.get_barrier_semaphore()
    for d in range(1, count):
        other = lax.rem(me + d, count)
        pl.semaphore_signal(
            barrier, 1, device_id=(pool_me, other), device_id_type=pl.DeviceIdType.MESH
        )
    pl.semaphore_wait(barrier, count - 1)
    copies = []
    for d in range(1, count):
        target = lax.rem(me + d, count)
        start = pl.multiple_of(target * rows, rows)
        copy = pltpu.make_async_remote_copy(
            src_ref=part_ref.at[:, pl.ds(start, rows), :],
            dst_ref=recv_ref.at[d - 1],
            send_sem=send_sems.at[d - 1],
            recv_sem=recv_sems.at[d - 1],
            device_id=(pool_me, target),
            device_id_type=pl.DeviceIdType.MESH,
        )
        copy.start()
        copies.append(copy)
    for copy in copies:
        copy.wait()


def scatter_rows(partial_value, count, rows):
    chunks, _, width = partial_value.shape
    return pl.pallas_call(
        functools.partial(scatter_kernel, count, rows),
        out_shape=jax.ShapeDtypeStruct((count - 1, chunks, rows, width), partial_value.dtype),
        in_specs=[pl.BlockSpec(memory_space=pl.ANY)],
        out_specs=pl.BlockSpec(memory_space=pl.ANY),
        scratch_shapes=[
            pltpu.SemaphoreType.DMA((count - 1,)),
            pltpu.SemaphoreType.DMA((count - 1,)),
        ],
        compiler_params=pltpu.CompilerParams(collective_id=0, has_side_effects=True),
    )(partial_value)


def shards(hidden, down_weight, adapter_shrink, adapter_expand, block_adapter, block_rows):
    input_rows, feat = hidden.shape
    block_count = block_adapter.shape[0]
    pool_count = lax.axis_size("pool")
    tensor_pos = lax.axis_index("tensor")
    tensor_count = lax.axis_size("tensor")
    side = 4
    quarter = pool_count // side
    my_y = tensor_pos // side
    my_x = tensor_pos % side
    own_rows = input_rows // tensor_count
    held, _, rank = adapter_shrink.shape
    column_span = adapter_expand.shape[1]
    width = down_weight.shape[1]

    pairs = []
    for p1 in range(pool_count):
        for y1 in range(side):
            for x1 in range(side):
                y2 = p1 % side
                p2 = (p1 // side) * side + (y2 - y1) % side
                pairs.append((p1 * tensor_count + y1 * side + x1, p2 * tensor_count + y2 * side + x1))
    moved = lax.ppermute(down_weight, ("pool", "tensor"), pairs)

    half = width // 2
    shrink_rows = held * feat * rank // half
    expand_rows = held * column_span * rank // half
    pack = jnp.concatenate(
        [
            moved[:, :half],
            adapter_shrink.reshape(shrink_rows, half),
            adapter_expand.reshape(expand_rows, half),
        ],
        axis=0,
    )
    gathered = lax.all_gather(pack, "pool", axis=0, tiled=False)
    pieces = [hidden] + [tensor_shift(hidden, side, s, True) for s in range(1, side)]
    hidden_column = jnp.stack(pieces, axis=0).reshape(side, side, side, own_rows, feat)
    hidden_column = jnp.transpose(hidden_column, (2, 0, 1, 3, 4)).reshape(
        side, side, side * own_rows, feat
    )
    hidden_padded = jnp.pad(
        hidden_column, ((0, 0), (0, 0), (0, 0), (0, pack.shape[0] - feat))
    )
    later, gathered, hidden_column, hidden_padded = lax.optimization_barrier(
        (moved[:, half:], gathered, hidden_column, hidden_padded)
    )
    plane_rows = gathered.shape[1]
    w_first = gathered.reshape(quarter, side, plane_rows, half)
    shrink_all = gathered[:, feat:feat + shrink_rows, :].reshape(
        pool_count * held, shrink_rows // held, half
    )
    expand_all = gathered[:, feat + shrink_rows:, :].reshape(
        pool_count * held, expand_rows // held, half
    )
    w_second = lax.all_gather(later, "pool", axis=0, tiled=False).reshape(
        quarter, side, feat, half
    )


    first = jnp.take(shrink_all, block_adapter, axis=0).reshape(block_count, feat, rank)
    second = jnp.take(expand_all, block_adapter, axis=0).reshape(block_count, column_span, rank)
    blocks = hidden.reshape(block_count, BLOCK, feat)
    shrink = jnp.einsum("bnf,bfr->bnr", blocks, first, preferred_element_type=jnp.float32)
    summed_shrink = tensor_allsum(shrink, side).astype(jnp.bfloat16)
    enlarged_rows = jnp.einsum(
        "bnr,bcr->bnc", summed_shrink, second, preferred_element_type=jnp.float32
    )
    delta = (adapter_scale_factor * enlarged_rows).astype(jnp.bfloat16).reshape(input_rows, column_span)

    def reduce_over_x(hidden_rows, w_half):
        def rows_for(owner_x):
            rows = lax.dynamic_index_in_dim(hidden_rows, owner_x, axis=0, keepdims=False)
            piece = jnp.einsum("sif,asfj->aij", rows, w_half, preferred_element_type=jnp.float32)
            return piece.astype(jnp.bfloat16).reshape(quarter, side, own_rows, half)

        summed = None
        for s in range(1, side):
            arrived = tensor_shift(rows_for((my_x + s) % side), side, s, False).astype(jnp.float32)
            summed = arrived if summed is None else summed + arrived
        return (summed + rows_for(my_x).astype(jnp.float32)).astype(jnp.bfloat16)

    order = (my_y - jnp.arange(side, dtype=jnp.int32)) % side

    def exchange_over_y(total):
        got = [lax.dynamic_index_in_dim(total, my_y, axis=1, keepdims=False)]
        for s in range(1, side):
            piece = lax.dynamic_index_in_dim(total, (my_y + s) % side, axis=1, keepdims=False)
            got.append(tensor_shift(piece, side, s, True))
        return jnp.transpose(jnp.take(jnp.stack(got, axis=0), order, axis=0), (2, 1, 0, 3))

    result = jnp.concatenate(
        [
            exchange_over_y(reduce_over_x(hidden_padded, w_first)),
            exchange_over_y(reduce_over_x(hidden_column, w_second)),
        ],
        axis=3,
    ).reshape(own_rows, pool_count * width)
    delta_mine = lax.all_to_all(delta, "tensor", split_axis=0, concat_axis=1, tiled=True)
    result = (result.astype(jnp.float32) + delta_mine.astype(jnp.float32)).astype(jnp.bfloat16)

    row_ids = tensor_pos * own_rows + jnp.arange(own_rows, dtype=jnp.int32)
    owning = (row_ids // BLOCK)[:, None] == jnp.arange(block_count, dtype=jnp.int32)[None, :]
    lengths = jnp.sum(jnp.where(owning, block_rows[None, :], 0), axis=1)
    valid = row_ids % BLOCK < lengths
    return jnp.where(valid[:, None], result, jnp.zeros_like(result))


def solution(mesh):
    in_specs = (
        P("pool", "tensor"),
        P("tensor", "pool"),
        P("pool", "tensor", None),
        P("pool", "tensor", None),
        P("pool"),
        P("pool"),
    )
    out_specs = P(("pool", "tensor"), None)
    return jax.shard_map(shards, mesh=mesh, in_specs=in_specs, out_specs=out_specs, check_vma=False)
```

```python
import functools

import jax
import jax.numpy as jnp
from jax import lax
from jax.experimental import pallas as pl
from jax.experimental.pallas import tpu as pltpu
from jax.sharding import PartitionSpec as P

BLOCK = 128


adapter_scale_factor = 0.5


def tensor_shift(x, side, step, along_y):
    perm = []
    for yy in range(side):
        for xx in range(side):
            if along_y:
                perm.append((yy * side + xx, ((yy + step) % side) * side + xx))
            else:
                perm.append((yy * side + xx, yy * side + (xx + step) % side))
    return lax.ppermute(x, "tensor", perm)


def tensor_allsum(x, side):
    for along_y in (False, True):
        x = x + sum(tensor_shift(x, side, s, along_y) for s in range(1, side))
    return x


def scatter_kernel(count, rows, part_ref, recv_ref, send_sems, recv_sems):
    me = lax.axis_index("tensor")
    pool_me = lax.axis_index("pool")
    barrier = pltpu.get_barrier_semaphore()
    for d in range(1, count):
        other = lax.rem(me + d, count)
        pl.semaphore_signal(
            barrier, 1, device_id=(pool_me, other), device_id_type=pl.DeviceIdType.MESH
        )
    pl.semaphore_wait(barrier, count - 1)
    copies = []
    for d in range(1, count):
        target = lax.rem(me + d, count)
        start = pl.multiple_of(target * rows, rows)
        copy = pltpu.make_async_remote_copy(
            src_ref=part_ref.at[:, pl.ds(start, rows), :],
            dst_ref=recv_ref.at[d - 1],
            send_sem=send_sems.at[d - 1],
            recv_sem=recv_sems.at[d - 1],
            device_id=(pool_me, target),
            device_id_type=pl.DeviceIdType.MESH,
        )
        copy.start()
        copies.append(copy)
    for copy in copies:
        copy.wait()


def scatter_rows(partial_value, count, rows):
    chunks, _, width = partial_value.shape
    return pl.pallas_call(
        functools.partial(scatter_kernel, count, rows),
        out_shape=jax.ShapeDtypeStruct((count - 1, chunks, rows, width), partial_value.dtype),
        in_specs=[pl.BlockSpec(memory_space=pl.ANY)],
        out_specs=pl.BlockSpec(memory_space=pl.ANY),
        scratch_shapes=[
            pltpu.SemaphoreType.DMA((count - 1,)),
            pltpu.SemaphoreType.DMA((count - 1,)),
        ],
        compiler_params=pltpu.CompilerParams(collective_id=0, has_side_effects=True),
    )(partial_value)


def shards(hidden, down_weight, adapter_shrink, adapter_expand, block_adapter, block_rows):
    input_rows, feat = hidden.shape
    block_count = block_adapter.shape[0]
    pool_count = lax.axis_size("pool")
    tensor_pos = lax.axis_index("tensor")
    tensor_count = lax.axis_size("tensor")
    side = 4
    quarter = pool_count // side
    my_y = tensor_pos // side
    my_x = tensor_pos % side
    own_rows = input_rows // tensor_count
    held, _, rank = adapter_shrink.shape
    column_span = adapter_expand.shape[1]
    width = down_weight.shape[1]

    pairs = []
    for p1 in range(pool_count):
        for y1 in range(side):
            for x1 in range(side):
                y2 = p1 % side
                p2 = (p1 // side) * side + (y2 - y1) % side
                pairs.append((p1 * tensor_count + y1 * side + x1, p2 * tensor_count + y2 * side + x1))
    moved = lax.ppermute(down_weight, ("pool", "tensor"), pairs)

    half = width // 2
    shrink_rows = held * feat * rank // half
    expand_rows = held * column_span * rank // half
    pack = jnp.concatenate(
        [
            moved[:, :half],
            adapter_shrink.reshape(shrink_rows, half),
            adapter_expand.reshape(expand_rows, half),
        ],
        axis=0,
    )
    gathered = lax.all_gather(pack, "pool", axis=0, tiled=False)
    pieces = [hidden] + [tensor_shift(hidden, side, s, True) for s in range(1, side)]
    hidden_column = jnp.stack(pieces, axis=0).reshape(side, side, side, own_rows, feat)
    hidden_column = jnp.transpose(hidden_column, (2, 0, 1, 3, 4)).reshape(
        side, side, side * own_rows, feat
    )
    hidden_padded = jnp.pad(
        hidden_column, ((0, 0), (0, 0), (0, 0), (0, pack.shape[0] - feat))
    )
    later, gathered, hidden_column, hidden_padded = lax.optimization_barrier(
        (moved[:, half:], gathered, hidden_column, hidden_padded)
    )
    plane_rows = gathered.shape[1]
    w_first = gathered.reshape(quarter, side, plane_rows, half)
    w_second = lax.all_gather(later, "pool", axis=0, tiled=False).reshape(
        quarter, side, feat, half
    )


    shrink_part = shrink_rows // held
    expand_part = expand_rows // held
    first = jnp.stack([
        lax.dynamic_slice(
            gathered,
            (block_adapter[b] // held, feat + (block_adapter[b] % held) * shrink_part, 0),
            (1, shrink_part, half),
        )[0]
        for b in range(block_count)
    ]).reshape(block_count, feat, rank)
    second = jnp.stack([
        lax.dynamic_slice(
            gathered,
            (block_adapter[b] // held, feat + shrink_rows + (block_adapter[b] % held) * expand_part, 0),
            (1, expand_part, half),
        )[0]
        for b in range(block_count)
    ]).reshape(block_count, column_span, rank)
    blocks = hidden.reshape(block_count, BLOCK, feat)
    shrink = jnp.einsum("bnf,bfr->bnr", blocks, first, preferred_element_type=jnp.float32)
    summed_shrink = tensor_allsum(shrink, side).astype(jnp.bfloat16)
    enlarged_rows = jnp.einsum(
        "bnr,bcr->bnc", summed_shrink, second, preferred_element_type=jnp.float32
    )
    delta = (adapter_scale_factor * enlarged_rows).astype(jnp.bfloat16).reshape(input_rows, column_span)

    def reduce_over_x(hidden_rows, w_half):
        def rows_for(owner_x):
            rows = lax.dynamic_index_in_dim(hidden_rows, owner_x, axis=0, keepdims=False)
            piece = jnp.einsum("sif,asfj->aij", rows, w_half, preferred_element_type=jnp.float32)
            return piece.astype(jnp.bfloat16).reshape(quarter, side, own_rows, half)

        summed = None
        for s in range(1, side):
            arrived = tensor_shift(rows_for((my_x + s) % side), side, s, False).astype(jnp.float32)
            summed = arrived if summed is None else summed + arrived
        return (summed + rows_for(my_x).astype(jnp.float32)).astype(jnp.bfloat16)

    order = (my_y - jnp.arange(side, dtype=jnp.int32)) % side

    def exchange_over_y(total):
        got = [lax.dynamic_index_in_dim(total, my_y, axis=1, keepdims=False)]
        for s in range(1, side):
            piece = lax.dynamic_index_in_dim(total, (my_y + s) % side, axis=1, keepdims=False)
            got.append(tensor_shift(piece, side, s, True))
        return jnp.transpose(jnp.take(jnp.stack(got, axis=0), order, axis=0), (2, 1, 0, 3))

    result = jnp.concatenate(
        [
            exchange_over_y(reduce_over_x(hidden_padded, w_first)),
            exchange_over_y(reduce_over_x(hidden_column, w_second)),
        ],
        axis=3,
    ).reshape(own_rows, pool_count * width)
    delta_mine = lax.all_to_all(delta, "tensor", split_axis=0, concat_axis=1, tiled=True)
    result = (result.astype(jnp.float32) + delta_mine.astype(jnp.float32)).astype(jnp.bfloat16)

    row_ids = tensor_pos * own_rows + jnp.arange(own_rows, dtype=jnp.int32)
    owning = (row_ids // BLOCK)[:, None] == jnp.arange(block_count, dtype=jnp.int32)[None, :]
    lengths = jnp.sum(jnp.where(owning, block_rows[None, :], 0), axis=1)
    valid = row_ids % BLOCK < lengths
    return jnp.where(valid[:, None], result, jnp.zeros_like(result))


def solution(mesh):
    in_specs = (
        P("pool", "tensor"),
        P("tensor", "pool"),
        P("pool", "tensor", None),
        P("pool", "tensor", None),
        P("pool"),
        P("pool"),
    )
    out_specs = P(("pool", "tensor"), None)
    return jax.shard_map(shards, mesh=mesh, in_specs=in_specs, out_specs=out_specs, check_vma=False)
```
